32 devices in a mesh: dp: 8 (over y, x, core), own: 4 (over z).
Axes of the slice: x: 2, y: 2, z: 4, core: 2. Of those that a mesh axis runs over, the one named last changes fastest.
Arguments:
- grads: bfloat16 [8, 6, 8192, 128], P('dp', None, 'own'), may hold values from -6 to 6
- proj: bfloat16 [4, 3, 8192, 1024], P('own', None, 'dp'), may hold values from -0.0625 to 0.0625
- moment1: float32 [4, 3, 1024, 128], P('own', None, 'dp'), may hold values from -24 to 24
- moment2: float32 [4, 3, 1024, 128], P('own', None, 'dp'), may hold values from 0.05 to 5
- plan: int32 [6], replicated, may hold values from 0 to 3, as said below
Outputs:
- update: bfloat16 [6, 8192, 128], P(None, 'own')
- new_moment1: float32 [4, 3, 1024, 128], P('own', None, 'dp')
- new_moment2: float32 [4, 3, 1024, 128], P('own', None, 'dp')
The draws below stay inside these ranges and needn't reach their ends.
Inputs may be any that keep to these rules, and one draw needn't show every extreme that they name: `plan`: no owner is named more than 3 times, and some owner is named exactly 3 times.
All inputs are finite; a program needn't handle non-finite values.
Results may differ from the reference program's by a relative error of at most 0.015.
Values may be sent and summed in bfloat16 or wider, within the bound.
A program may use at most 64 MiB of HBM per device.

```python
import math
import jax
import jax.numpy as jnp
from jax import lax

D = 8192
RANK = 1024
COLS = 128
CAP = 3
MATS = 6
N_DP = 8
N_OWN = 4


def draw_plan(key, part):
    places = N_OWN * CAP
    key_score, key_full, key_order = jax.random.split(key, 3)
    scores = jax.random.randint(key_score, (places,), 0, 1000)
    favored = jax.random.randint(key_full, (), 0, N_OWN)
    owners = jnp.arange(places, dtype=jnp.int32) // CAP
    ranked = scores * places + jnp.arange(places, dtype=jnp.int32) + jnp.where(owners == favored, 1000 * places, 0)
    chosen = jnp.argsort(-ranked, stable=True)[:MATS]
    picked = owners[chosen]
    shuffle = jax.random.permutation(key_order, MATS)
    return picked[shuffle].astype(jnp.int32)


def block_levels(stream_key, extent, pieces, low, high):
    def one(axis_at, blocks):
        heights = jax.random.uniform(jax.random.fold_in(jax.random.fold_in(stream_key, 6), axis_at), (blocks,), jnp.float32, low / len(pieces), high / len(pieces))
        return jnp.repeat(jnp.exp(heights), extent[axis_at] // blocks).reshape((-1,) + (1,) * (len(extent) - axis_at - 1))

    level = one(*pieces[0])
    for cut in pieces[1:]:
        level = level * one(*cut)
    return level


def scatter_about(stream_key, dims, scale, limit, pieces=(), kind=jnp.bfloat16):
    array = jax.random.normal(stream_key, dims, jnp.float32) * scale
    if len(pieces) > 0:
        array = block_levels(stream_key, dims, pieces, -0.22, 0.18) * array
    return jnp.clip(array, min=-limit, max=limit).astype(kind)


def setup_inputs(seed: int = 0) -> dict:
    key_list = jax.random.split(jax.random.key(seed), 6)
    return {
        "grads": scatter_about(key_list[0], (N_DP, MATS, D, COLS), 1.0, 6.0, ((0, 8), (2, 4))),
        "proj": scatter_about(key_list[1], (N_OWN, CAP, D, RANK), D ** -0.5, 0.0625, ((0, 4), (2, 8))),
        "moment1": scatter_about(key_list[2], (N_OWN, CAP, RANK, COLS), 4.0, 24.0, ((0, 4), (2, 8)), jnp.float32),
        "moment2": jnp.clip(jnp.exp(math.log(5.0) - 4.6051702 * jax.random.uniform(key_list[3], (N_OWN, CAP, RANK, COLS), jnp.float32) ** block_levels(key_list[3], (N_OWN, CAP, RANK, COLS), ((0, 4), (2, 8)), -0.2, 0.2)), 0.05, 5.0),
        "plan": draw_plan(jax.random.fold_in(key_list[5], 71), 0),
    }


beta_one = 0.9
beta_two = 0.999
adam_eps = 1e-08
norm_eps = 1e-06
correct_one = 1.0 - 0.9 ** 10
correct_two = 1.0 - 0.999 ** 10

def slot_selector(plan):
    matrices = plan.shape[0]
    places = jnp.arange(N_OWN * CAP, dtype=jnp.int32)
    owners = places // CAP
    within = places % CAP
    index = jnp.arange(matrices, dtype=jnp.int32)
    before = lax.optimization_barrier(jnp.sum(((plan[None, :] == plan[:, None]) & (index[None, :] < index[:, None])).astype(jnp.int32), axis=1))
    chosen = (plan[None, :] == owners[:, None]) & (before[None, :] == within[:, None])
    return chosen.astype(jnp.float32)

def reference(grads, proj, moment1, moment2, plan):
    selector = slot_selector(plan)
    total = lax.optimization_barrier(jnp.sum(grads.astype(jnp.float32), axis=0))
    slot_grad = jnp.einsum('sj,jdc->sdc', selector, total)
    grad_half = lax.optimization_barrier(slot_grad.astype(jnp.bfloat16))
    projection = proj.reshape(N_OWN * CAP, D, RANK).astype(jnp.float32)
    rank_grad = jnp.einsum('sdr,sdc->src', projection, grad_half.astype(jnp.float32))
    first_old = moment1.reshape(N_OWN * CAP, RANK, COLS)
    second_old = moment2.reshape(N_OWN * CAP, RANK, COLS)
    first_new = beta_one * first_old + (1.0 - beta_one) * rank_grad
    second_new = beta_two * second_old + (1.0 - beta_two) * rank_grad * rank_grad
    adam_step = first_new / correct_one / (jnp.sqrt(second_new / correct_two) + adam_eps)
    adam_half = lax.optimization_barrier(adam_step.astype(jnp.bfloat16)).astype(jnp.float32)
    rank_half = lax.optimization_barrier(rank_grad.astype(jnp.bfloat16)).astype(jnp.float32)
    grad_norms = lax.optimization_barrier(jnp.sum(rank_grad * rank_grad, axis=1))
    step_norms = lax.optimization_barrier(jnp.sum(adam_half * adam_half, axis=1))
    column_scale = jnp.sqrt(step_norms) / (jnp.sqrt(grad_norms) + norm_eps)
    combined = lax.optimization_barrier((adam_half - column_scale[:, None, :] * rank_half).astype(jnp.bfloat16))
    slot_update = jnp.einsum('sdr,src->sdc', projection, combined.astype(jnp.float32)) + column_scale[:, None, :] * slot_grad
    update_half = lax.optimization_barrier(slot_update.astype(jnp.bfloat16))
    update = jnp.einsum('sj,sdc->jdc', selector, update_half.astype(jnp.float32)).astype(jnp.bfloat16)
    return (update, first_new.reshape(N_OWN, CAP, RANK, COLS), second_new.reshape(N_OWN, CAP, RANK, COLS))
```

```python
import functools
import jax
import jax.numpy as jnp
from jax import lax
from jax.experimental import pallas as pl
from jax.experimental.pallas import tpu as pltpu
from jax.sharding import PartitionSpec as P

beta_one = 0.9
beta_two = 0.999
adam_eps = 1e-08
norm_eps = 1e-06
correct_one = 1.0 - 0.9**10
correct_two = 1.0 - 0.999**10

OUT_CHUNKS = (4, 1, 1)
BACK_CHUNKS = 2
F32 = jnp.float32
BF16 = jnp.bfloat16
MESH = pl.DeviceIdType.MESH


def places_of(plan, mats):
    owner = [plan[j] for j in range(mats)]
    within = []
    for j in range(mats):
        before = jnp.int32(0)
        for i in range(j):
            before = before + jnp.where(owner[i] == owner[j], 1, 0)
        within.append(before)
    position = []
    for j in range(mats):
        ahead = jnp.int32(0)
        for i in range(mats):
            if i < j:
                ahead = ahead + jnp.where(within[i] <= within[j], 1, 0)
            elif i > j:
                ahead = ahead + jnp.where(within[i] < within[j], 1, 0)
        position.append(ahead)
    return owner, within, position


def kernel(
    n, m, plan, grads, proj, m1_ref, m2_ref, gathered, m1_out, m2_out,
    held_core, held_other, pair_out, pair_in, half_sum, chip_in, total, slot_out, grad, weights,
    part, part_in, pair_sum, share_in, norms, norms_in, mixed, update, row_in, plane_in, picked,
    old, moments,
    load_sem, moment_sem, local_sem,
    s_pair, r_pair, s_chip, r_chip, s_slot, r_slot,
    s_part, r_part, s_share, r_share, s_norm, r_norm, s_mix, r_mix, s_mixf, r_mixf,
    s_back, r_back, s_home, r_home, s_out, r_out, s_outf, r_outf,
):
    mats = grads.shape[0]
    chips = n // 2
    piece = grads.shape[3]
    cap = m1_ref.shape[0]
    rank_rows = m1_ref.shape[1]
    cols = m1_ref.shape[2]
    rank = n * rank_rows
    dp = lax.axis_index("dp")
    own = lax.axis_index("own")
    core = lax.rem(dp, 2)
    chip = lax.div(dp, 2)
    other = 1 - core
    partner = (2 * chip + other, own)
    out_ends = out_bounds(mats, cap, m)
    back_ends = back_bounds(mats, cap)
    out_ranges = list(zip([0] + out_ends[:-1], out_ends))
    back_ranges = list(zip([0] + back_ends[:-1], back_ends))

    def at_chip(which):
        return (2 * which + core, own)

    def remote(src, dst, send, recv, device):
        return pltpu.make_async_remote_copy(
            src_ref=src, dst_ref=dst, send_sem=send, recv_sem=recv,
            device_id=device, device_id_type=MESH,
        )

    def rows(ch, count):
        size = piece // count
        return pl.ds(ch * size, size)

    barrier = pltpu.get_barrier_semaphore()

    greeted = [(dp, lax.rem(own + d, m)) for d in range(1, m)]
    greeted += [at_chip(lax.rem(chip + d, chips)) for d in range(1, chips)] + [partner]
    for device in greeted:
        pl.semaphore_signal(barrier, inc=1, device_id=device, device_id_type=MESH)

    load_other = pltpu.make_async_copy(grads.at[:, other], held_other, load_sem.at[0])
    load_other.start()
    load_core = pltpu.make_async_copy(grads.at[:, core], held_core, load_sem.at[1])
    load_core.start()
    load_proj = pltpu.make_async_copy(proj, weights, load_sem.at[2])
    load_proj.start()
    load_old = [
        pltpu.make_async_copy(m1_ref, old.at[0], load_sem.at[3]),
        pltpu.make_async_copy(m2_ref, old.at[1], load_sem.at[4]),
    ]
    for c in load_old:
        c.start()

    owner, within, position = places_of(plan, mats)
    order = []
    for p in range(mats):
        index = jnp.int32(0)
        for j in range(mats):
            index = jnp.where(position[j] == p, j, index)
        order.append(index)

    def occupant(plane, k):
        at = jnp.int32(0)
        valid = jnp.int32(0)
        for j in range(mats):
            here = jnp.logical_and(owner[j] == plane, within[j] == k)
            at = jnp.where(here, position[j], at)
            valid = jnp.where(here, 1, valid)
        return at, valid.astype(F32)

    sends = []
    guarded = []
    out_units = [(g, ch) for g in range(cap) for ch in range(OUT_CHUNKS[g])]

    load_other.wait()
    pair = {}
    first_unit = True
    for g, ch in out_units:
        at = rows(ch, OUT_CHUNKS[g])
        lo, hi = out_ranges[g]
        for p in range(lo, hi):
            pair_out[p, :, at] = held_other[order[p], :, at]
        if first_unit:
            pl.semaphore_wait(barrier, len(greeted))
            first_unit = False
        c = remote(
            pair_out.at[lo:hi, :, at], pair_in.at[lo:hi, :, at],
            s_pair[g].at[ch], r_pair[g].at[ch], partner,
        )
        c.start()
        pair[g, ch] = c
    sends += list(pair.values())

    load_core.wait()
    over = {}
    for g, ch in out_units:
        count = OUT_CHUNKS[g]
        at = rows(ch, count)
        lo, hi = out_ranges[g]
        pair[g, ch].wait_recv()
        for p in range(lo, hi):

            @pl.loop(0, chips)
            def _(t):
                half_sum[t, p, at] = (
                    held_core[order[p], t, at].astype(F32) + pair_in[p, t, at].astype(F32)
                ).astype(BF16)

        for d in range(1, chips):
            to = lax.rem(chip + d, chips)
            c = remote(
                half_sum.at[to, lo:hi, at], chip_in.at[d - 1, lo:hi, at],
                s_chip[g].at[ch, d], r_chip[g].at[ch, d], at_chip(to),
            )
            c.start()
            over[g, ch, d] = c
    sends += list(over.values())

    def out_step(g, ch):
        count = OUT_CHUNKS[g]
        at = rows(ch, count)
        lo, hi = out_ranges[g]
        for d in range(1, chips):
            over[g, ch, d].wait_recv()
        for p in range(lo, hi):
            acc = half_sum[chip, p, at].astype(F32)
            for d in range(1, chips):
                acc = acc + chip_in[d - 1, p, at].astype(F32)
            total[p, at] = acc.astype(BF16)
        for z in range(m):
            index, valid = occupant(z, g)
            slot_out[g, z, at] = (total[index, at].astype(F32) * valid).astype(BF16)
            c = remote(
                slot_out.at[g, z, at], grad.at[g, chip, at],
                s_slot[g].at[ch, z], r_slot[g].at[ch, chip], (2 * own + core, z),
            )
            mine = jnp.logical_and(own == z, chip == own)

            @pl.when(jnp.logical_not(mine))
            def _():
                c.start()

            @pl.when(mine)
            def _():
                grad[g, chip, at] = slot_out[g, z, at]

            guarded.append((jnp.logical_not(mine), c))

    parts = {}
    shares = {}
    across = {}
    rank_half = {}
    adam = {}
    scale = {}
    mix = {}
    forward = {}
    back = {}
    home = {}
    gather = {}
    handed = {}
    copies = []

    def project(k):
        count = OUT_CHUNKS[k]
        for ch in range(count):
            for source in range(chips):
                at = rows(ch, count)
                c = remote(
                    slot_out.at[k, 0, at], grad.at[k, source, at],
                    s_slot[k].at[ch, 0], r_slot[k].at[ch, source], (dp, own),
                )

                @pl.when(jnp.logical_not(jnp.logical_and(chip == own, source == chip)))
                def _():
                    c.wait_recv()

        g = grad[k].reshape(chips * piece, cols)
        w = weights[k].reshape(chips * piece, rank)
        value = lax.dot_general(g, w, (((0,), (0,)), ((), ())), preferred_element_type=F32)
        value = value.T.astype(BF16)
        for t in range(chips):
            for s in range(2):
                at = (2 * t + s) * rank_rows
                part[s, k, t] = value[at : at + rank_rows]
        c = remote(part.at[other, k], part_in.at[k], s_part.at[k], r_part.at[k], partner)
        c.start()
        parts[k] = c
        sends.append(c)

    def share(k):
        parts[k].wait_recv()
        for t in range(chips):
            pair_sum[k, t] = (part[core, k, t].astype(F32) + part_in[k, t].astype(F32)).astype(BF16)
        for d in range(1, chips):
            to = lax.rem(chip + d, chips)
            c = remote(
                pair_sum.at[k, to], share_in.at[k, d - 1],
                s_share.at[k, d], r_share.at[k, d], at_chip(to),
            )
            c.start()
            shares[k, d] = c
            sends.append(c)

    def step(k):
        for d in range(1, chips):
            shares[k, d].wait_recv()
        value = pair_sum[k, chip].astype(F32)
        for d in range(1, chips):
            value = value + share_in[k, d - 1].astype(F32)
        first = beta_one * old[0, k] + (1.0 - beta_one) * value
        second = beta_two * old[1, k] + (1.0 - beta_two) * value * value
        moments[0, k] = first
        moments[1, k] = second
        taken = first / correct_one / (jnp.sqrt(second / correct_two) + adam_eps)
        taken = taken.astype(BF16)
        wide = taken.astype(F32)
        norms[k, 0] = jnp.sum(value * value, axis=0, keepdims=True)
        norms[k, 1] = jnp.sum(wide * wide, axis=0, keepdims=True)
        rank_half[k] = value.astype(BF16)
        adam[k] = taken
        for d in range(1, n):
            c = remote(
                norms.at[k], norms_in.at[d - 1, k], s_norm.at[k, d], r_norm.at[k, d],
                (lax.rem(dp + d, n), own),
            )
            c.start()
            across[k, d] = c
            sends.append(c)
        for i, target in ((0, m1_out), (1, m2_out)):
            c = pltpu.make_async_copy(moments.at[i, k], target.at[k], moment_sem.at[i, k])
            c.start()
            copies.append(c)

    def mix_step(k):
        for d in range(1, n):
            across[k, d].wait_recv()
        grad_sum = norms[k, 0]
        step_sum = norms[k, 1]
        for d in range(1, n):
            grad_sum = grad_sum + norms_in[d - 1, k, 0]
            step_sum = step_sum + norms_in[d - 1, k, 1]
        scale[k] = jnp.sqrt(step_sum) / (jnp.sqrt(grad_sum) + norm_eps)
        mixed[k, dp] = (adam[k].astype(F32) - scale[k] * rank_half[k].astype(F32)).astype(BF16)
        for d in range(1, chips):
            to = lax.rem(chip + d, chips)
            c = remote(mixed.at[k, dp], mixed.at[k, dp], s_mix.at[k, d], r_mix.at[k, d], at_chip(to))
            c.start()
            mix[k, d] = c
            sends.append(c)
        c = remote(mixed.at[k, dp], mixed.at[k, dp], s_mixf.at[k, 0], r_mixf.at[k, 0], partner)
        c.start()
        forward[k, 0] = c
        sends.append(c)

    def mix_forward(k):
        for d in range(1, chips):
            mix[k, d].wait_recv()
            at = 2 * lax.rem(chip + chips - d, chips) + core
            c = remote(mixed.at[k, at], mixed.at[k, at], s_mixf.at[k, d], r_mixf.at[k, d], partner)
            c.start()
            forward[k, d] = c
            sends.append(c)

    def spread(k):
        for d in range(chips):
            forward[k, d].wait_recv()
        count = BACK_CHUNKS
        size = piece // count
        c_full = mixed[k].reshape(rank, cols)
        for ch in range(count):
            at = rows(ch, count)
            w = weights[k, :, at].reshape(chips * size, rank)
            value = jnp.dot(w, c_full, preferred_element_type=F32)
            g = grad[k, :, at].reshape(chips * size, cols).astype(F32)
            value = (value + scale[k] * g).astype(BF16)
            for t in range(chips):
                update[k, t, at] = value[t * size : (t + 1) * size]
            for d in range(1, chips):
                to = lax.rem(chip + d, chips)
                c = remote(
                    update.at[k, to, at], row_in.at[k, chip, at],
                    s_back[k].at[ch, d], r_back[k].at[ch, d], at_chip(to),
                )
                c.start()
                back[k, ch, d] = c
                sends.append(c)
            row_in[k, chip, at] = update[k, chip, at]

    def go_home(k, ch):
        at = rows(ch, BACK_CHUNKS)
        for d in range(1, chips):
            back[k, ch, d].wait_recv()
        for dz in range(1, m):
            to = lax.rem(own + dz, m)
            c = remote(
                row_in.at[k, to, at], plane_in[k][ch].at[own],
                s_home[k].at[ch, dz], r_home[k].at[ch, dz], (dp, to),
            )
            c.start()
            home[k, ch, dz] = c
            sends.append(c)
        plane_in[k][ch][own] = row_in[k, own, at]

    def pick(k, ch):
        count = BACK_CHUNKS
        at = rows(ch, count)
        for dz in range(1, m):
            home[k, ch, dz].wait_recv()
        lo, hi = back_ranges[k]
        for p in range(lo, hi):
            who = jnp.int32(0)
            slot = jnp.int32(0)
            for j in range(mats):
                who = jnp.where(position[j] == p, owner[j], who)
                slot = jnp.where(position[j] == p, within[j], slot)
            value = plane_in[0][ch][who]
            for i in range(1, k + 1):
                value = jnp.where(slot == i, plane_in[i][ch][who], value)
            picked[p, at] = value
        for d in range(1, chips):
            to = lax.rem(chip + d, chips)
            c = remote(
                picked.at[lo:hi, at], gathered.at[lo:hi, core, chip, at],
                s_out[k].at[ch, d], r_out[k].at[ch, d], at_chip(to),
            )
            c.start()
            gather[k, ch, d] = c
        c = remote(
            picked.at[lo:hi, at], gathered.at[lo:hi, core, chip, at],
            s_outf[k].at[ch, 0], r_outf[k].at[ch, 0], partner,
        )
        c.start()
        handed[k, ch, 0] = c
        c = pltpu.make_async_copy(
            picked.at[lo:hi, at], gathered.at[lo:hi, core, chip, at], local_sem[k].at[ch]
        )
        c.start()
        copies.append(c)

    def hand(k, ch):
        at = rows(ch, BACK_CHUNKS)
        lo, hi = back_ranges[k]
        for d in range(1, chips):
            gather[k, ch, d].wait_recv()
            source = lax.rem(chip + chips - d, chips)
            block = gathered.at[lo:hi, core, source, at]
            c = remote(block, block, s_outf[k].at[ch, d], r_outf[k].at[ch, d], partner)
            c.start()
            handed[k, ch, d] = c

    tasks = {
        "o": out_step, "p": project, "s": share, "a": step, "n": mix_step, "f": mix_forward,
        "u": spread, "h": go_home, "k": pick, "g": hand,
    }
    for name, k in ORDER:
        if name == "o":
            for ch in range(OUT_CHUNKS[k]):
                out_step(k, ch)
        elif name == "p":
            if k == 0:
                load_proj.wait()
                for c in load_old:
                    c.wait()
            project(k)
        elif name in "hkg":
            for ch in range(BACK_CHUNKS):
                tasks[name](k, ch)
        else:
            tasks[name](k)

    for c in handed.values():
        c.wait_recv()
    sends += list(gather.values()) + list(handed.values())
    for c in copies:
        c.wait()
    for c in sends:
        c.wait_send()
    for sent, c in guarded:

        @pl.when(sent)
        def _():
            c.wait_send()


def out_bounds(mats, cap, owners):
    ends = [min(mats - cap + 1, owners)]
    for k in range(1, cap):
        ends.append(min(mats - cap + 1 + k, owners * (k + 1)))
    ends[-1] = mats
    return ends


def back_bounds(mats, cap):
    return [-(-mats * (k + 1) // cap) for k in range(cap)]


ORDER = (
    ("o", 0), ("o", 1), ("o", 2), ("p", 0), ("s", 0), ("p", 1), ("a", 0), ("s", 1), ("p", 2), ("n", 0),
    ("a", 1), ("s", 2), ("f", 0), ("n", 1), ("u", 0), ("a", 2), ("f", 1), ("h", 0), ("u", 1), ("n", 2),
    ("h", 1), ("k", 0), ("f", 2), ("u", 2), ("k", 1), ("g", 0), ("h", 2), ("g", 1), ("k", 2), ("g", 2),
)


def settle(plan, gathered, first, second, out, first_out, second_out, sem):
    mats = out.shape[0]
    _, _, position = places_of(plan, mats)
    copies = []
    for j in range(mats):
        copies.append(pltpu.make_async_copy(gathered.at[position[j]], out.at[j], sem.at[j]))
    copies.append(pltpu.make_async_copy(first, first_out, sem.at[mats]))
    copies.append(pltpu.make_async_copy(second, second_out, sem.at[mats + 1]))
    for c in copies:
        c.start()
    for c in copies:
        c.wait()


def local(grads, proj, moment1, moment2, plan):
    n = lax.axis_size("dp")
    m = lax.axis_size("own")
    chips = n // 2
    mats, own_rows, cols = grads.shape[1:]
    cap, held_rows, rank = proj.shape[1:]
    rank_rows = moment1.shape[2]
    piece = held_rows // chips
    g = grads.reshape(mats, 2, chips, piece, cols)
    w = proj.reshape(cap, chips, piece, rank)
    hbm = pl.BlockSpec(memory_space=pltpu.HBM)
    smem = pl.BlockSpec(memory_space=pltpu.SMEM)
    anywhere = pl.BlockSpec(memory_space=pl.ANY)
    dma = pltpu.SemaphoreType.DMA
    share = (cap, rank_rows, cols)
    oc, bc = OUT_CHUNKS, (BACK_CHUNKS,) * cap

    def per_slot(counts, *shape):
        return [dma((c,) + shape) for c in counts]

    outs = (
        jax.ShapeDtypeStruct(g.shape, BF16),
        jax.ShapeDtypeStruct(share, F32),
        jax.ShapeDtypeStruct(share, F32),
    )
    gathered, first, second = pl.pallas_call(
        functools.partial(kernel, n, m),
        out_shape=outs,
        in_specs=[smem, hbm, hbm, hbm, hbm],
        out_specs=(anywhere, anywhere, anywhere),
        scratch_shapes=[
            pltpu.VMEM((mats, chips, piece, cols), BF16),
            pltpu.VMEM((mats, chips, piece, cols), BF16),
            pltpu.VMEM((mats, chips, piece, cols), BF16),
            pltpu.VMEM((mats, chips, piece, cols), BF16),
            pltpu.VMEM((chips, mats, piece, cols), BF16),
            pltpu.VMEM((chips - 1, mats, piece, cols), BF16),
            pltpu.VMEM((mats, piece, cols), BF16),
            pltpu.VMEM((cap, m, piece, cols), BF16),
            pltpu.VMEM((cap, chips, piece, cols), BF16),
            pltpu.VMEM((cap, chips, piece, rank), BF16),
            pltpu.VMEM((2, cap, chips, rank_rows, cols), BF16),
            pltpu.VMEM((cap, chips, rank_rows, cols), BF16),
            pltpu.VMEM((cap, chips, rank_rows, cols), BF16),
            pltpu.VMEM((cap, chips - 1, rank_rows, cols), BF16),
            pltpu.VMEM((cap, 2, 1, cols), F32),
            pltpu.VMEM((n - 1, cap, 2, 1, cols), F32),
            pltpu.VMEM((cap, n, rank_rows, cols), BF16),
            pltpu.VMEM((cap, chips, piece, cols), BF16),
            pltpu.VMEM((cap, chips, piece, cols), BF16),
            [[pltpu.VMEM((m, piece // BACK_CHUNKS, cols), BF16)] * BACK_CHUNKS] * cap,
            pltpu.VMEM((mats, piece, cols), BF16),
            pltpu.VMEM((2, cap, rank_rows, cols), F32),
            pltpu.VMEM((2, cap, rank_rows, cols), F32),
            dma((5,)), dma((2, cap)), per_slot(bc),
            per_slot(oc), per_slot(oc),
            per_slot(oc, chips), per_slot(oc, chips),
            per_slot(oc, m), per_slot(oc, chips),
            dma((cap,)), dma((cap,)),
            dma((cap, chips)), dma((cap, chips)),
            dma((cap, n)), dma((cap, n)),
            dma((cap, chips)), dma((cap, chips)),
            dma((cap, chips)), dma((cap, chips)),
            per_slot(bc, chips), per_slot(bc, chips),
            per_slot(bc, m), per_slot(bc, m),
            per_slot(bc, chips), per_slot(bc, chips),
            per_slot(bc, chips), per_slot(bc, chips),
        ],
        compiler_params=pltpu.CompilerParams(
            collective_id=0, has_side_effects=True, vmem_limit_bytes=44 * 2**20
        ),
    )(plan, *(pltpu.with_memory_space_constraint(x, pltpu.HBM) for x in (g, w, moment1[0], moment2[0])))
    update, first, second = pl.pallas_call(
        settle,
        out_shape=outs,
        in_specs=[smem, anywhere, anywhere, anywhere],
        out_specs=(anywhere, anywhere, anywhere),
        scratch_shapes=[dma((mats + 2,))],
        compiler_params=pltpu.CompilerParams(vmem_limit_bytes=2**20),
    )(plan, gathered, first, second)
    return (update.reshape(mats, own_rows, cols), first[None], second[None])


def solution(mesh):
    return jax.shard_map(
        local,
        mesh=mesh,
        in_specs=(
            P("dp", None, "own", None),
            P("own", None, "dp", None),
            P("own", None, "dp", None),
            P("own", None, "dp", None),
            P(),
        ),
        out_specs=(P(None, "own", None), P("own", None, "dp", None), P("own", None, "dp", None)),
        check_vma=False,
    )
```

```python
import functools
import jax
import jax.numpy as jnp
from jax import lax
from jax.experimental import pallas as pl
from jax.experimental.pallas import tpu as pltpu
from jax.sharding import PartitionSpec as P

beta_one = 0.9
beta_two = 0.999
adam_eps = 1e-08
norm_eps = 1e-06
correct_one = 1.0 - 0.9**10
correct_two = 1.0 - 0.999**10

OUT_CHUNKS = (4, 1, 1)
BACK_CHUNKS = 2
F32 = jnp.float32
BF16 = jnp.bfloat16
MESH = pl.DeviceIdType.MESH


def places_of(plan, mats):
    owner = [plan[j] for j in range(mats)]
    within = []
    for j in range(mats):
        before = jnp.int32(0)
        for i in range(j):
            before = before + jnp.where(owner[i] == owner[j], 1, 0)
        within.append(before)
    position = []
    for j in range(mats):
        ahead = jnp.int32(0)
        for i in range(mats):
            if i < j:
                ahead = ahead + jnp.where(within[i] <= within[j], 1, 0)
            elif i > j:
                ahead = ahead + jnp.where(within[i] < within[j], 1, 0)
        position.append(ahead)
    return owner, within, position


def kernel(
    n, m, plan, grads, proj, m1_ref, m2_ref, gathered, m1_out, m2_out,
    held_core, held_other, pair_out, pair_in, half_sum, chip_in, total, slot_out, grad, weights,
    part, part_in, pair_sum, share_in, mixed, update, row_in, plane_in, picked,
    old, moments,
    load_sem, moment_sem, local_sem,
    s_pair, r_pair, s_chip, r_chip, s_slot, r_slot,
    s_part, r_part, s_share, r_share, s_mix, r_mix, s_mixf, r_mixf,
    s_back, r_back, s_home, r_home, s_out, r_out, s_diag, r_diag, s_outf, r_outf,
):
    mats = grads.shape[0]
    chips = n // 2
    piece = grads.shape[3]
    cap = m1_ref.shape[0]
    rank_rows = m1_ref.shape[1]
    cols = m1_ref.shape[2]
    rank = n * rank_rows
    dp = lax.axis_index("dp")
    own = lax.axis_index("own")
    core = lax.rem(dp, 2)
    chip = lax.div(dp, 2)
    other = 1 - core
    partner = (2 * chip + other, own)
    out_ends = out_bounds(mats, cap, m)
    back_ends = back_bounds(mats, cap)
    out_ranges = list(zip([0] + out_ends[:-1], out_ends))
    back_ranges = list(zip([0] + back_ends[:-1], back_ends))

    def at_chip(which):
        return (2 * which + core, own)

    square = chips == 4
    reach = (1, 2) if square else tuple(range(1, chips))

    def away(d):
        if not square:
            return lax.rem(chip + d, chips)
        return chip + 1 - 2 * lax.rem(chip, 2) if d == 1 else lax.rem(chip + 2, chips)

    def from_(d):
        return away(d) if square else lax.rem(chip + chips - d, chips)

    def remote(src, dst, send, recv, device):
        return pltpu.make_async_remote_copy(
            src_ref=src, dst_ref=dst, send_sem=send, recv_sem=recv,
            device_id=device, device_id_type=MESH,
        )

    def rows(ch, count):
        size = piece // count
        return pl.ds(ch * size, size)

    barrier = pltpu.get_barrier_semaphore()

    def plane_at(i):
        h = m // 2
        half = lax.div(own, h)
        if i < m - h:
            return (1 - half) * h + lax.rem(own + i, h)
        return half * h + lax.rem(own + i - h + 1, h)

    greeted = [(dp, lax.rem(own + d, m)) for d in range(1, m)]
    greeted += [at_chip(lax.rem(chip + d, chips)) for d in range(1, chips)] + [partner]
    for device in greeted:
        pl.semaphore_signal(barrier, inc=1, device_id=device, device_id_type=MESH)

    load_other = pltpu.make_async_copy(grads.at[:, other], held_other, load_sem.at[0])
    load_other.start()
    load_core = pltpu.make_async_copy(grads.at[:, core], held_core, load_sem.at[1])
    load_core.start()
    load_proj = pltpu.make_async_copy(proj, weights, load_sem.at[2])
    load_proj.start()
    load_old = [
        pltpu.make_async_copy(m1_ref, old.at[0], load_sem.at[3]),
        pltpu.make_async_copy(m2_ref, old.at[1], load_sem.at[4]),
    ]
    for c in load_old:
        c.start()

    owner, within, position = places_of(plan, mats)
    order = []
    for p in range(mats):
        index = jnp.int32(0)
        for j in range(mats):
            index = jnp.where(position[j] == p, j, index)
        order.append(index)

    def occupant(plane, k):
        at = jnp.int32(0)
        valid = jnp.int32(0)
        for j in range(mats):
            here = jnp.logical_and(owner[j] == plane, within[j] == k)
            at = jnp.where(here, position[j], at)
            valid = jnp.where(here, 1, valid)
        return at, valid.astype(F32)

    sends = []
    guarded = []
    out_units = [(g, ch) for g in range(cap) for ch in range(OUT_CHUNKS[g])]

    load_other.wait()
    pair = {}
    first_unit = True
    for g, ch in out_units:
        at = rows(ch, OUT_CHUNKS[g])
        lo, hi = out_ranges[g]
        for p in range(lo, hi):
            pair_out[p, :, at] = held_other[order[p], :, at]
        if first_unit:
            pl.semaphore_wait(barrier, len(greeted))
            first_unit = False
        c = remote(
            pair_out.at[lo:hi, :, at], pair_in.at[lo:hi, :, at],
            s_pair[g].at[ch], r_pair[g].at[ch], partner,
        )
        c.start()
        pair[g, ch] = c
    sends += list(pair.values())

    load_core.wait()
    over = {}
    for g, ch in out_units:
        count = OUT_CHUNKS[g]
        at = rows(ch, count)
        lo, hi = out_ranges[g]
        pair[g, ch].wait_recv()
        for p in range(lo, hi):

            @pl.loop(0, chips)
            def _(t):
                half_sum[t, p, at] = (
                    held_core[order[p], t, at].astype(F32) + pair_in[p, t, at].astype(F32)
                ).astype(BF16)

        for d in range(1, chips):
            to = lax.rem(chip + d, chips)
            c = remote(
                half_sum.at[to, lo:hi, at], chip_in.at[d - 1, lo:hi, at],
                s_chip[g].at[ch, d], r_chip[g].at[ch, d], at_chip(to),
            )
            c.start()
            over[g, ch, d] = c
    sends += list(over.values())

    def out_step(g, ch):
        count = OUT_CHUNKS[g]
        at = rows(ch, count)
        lo, hi = out_ranges[g]
        for d in range(1, chips):
            over[g, ch, d].wait_recv()
        for p in range(lo, hi):
            acc = half_sum[chip, p, at].astype(F32)
            for d in range(1, chips):
                acc = acc + chip_in[d - 1, p, at].astype(F32)
            total[p, at] = acc.astype(BF16)
        for i in range(m):
            z = plane_at(i)
            index, valid = occupant(z, g)
            slot_out[g, z, at] = (total[index, at].astype(F32) * valid).astype(BF16)
            c = remote(
                slot_out.at[g, z, at], grad.at[g, chip, at],
                s_slot[g].at[ch, i], r_slot[g].at[ch, chip], (2 * own + core, z),
            )
            mine = jnp.logical_and(own == z, chip == own)

            @pl.when(jnp.logical_not(mine))
            def _():
                c.start()

            @pl.when(mine)
            def _():
                grad[g, chip, at] = slot_out[g, z, at]

            guarded.append((jnp.logical_not(mine), c))

    parts = {}
    shares = {}
    combined = {}
    scale = {}
    mix = {}
    forward = {}
    back = {}
    home = {}
    gather = {}
    handed = {}
    copies = []

    def project(k):
        count = OUT_CHUNKS[k]
        for ch in range(count):
            for source in range(chips):
                at = rows(ch, count)
                c = remote(
                    slot_out.at[k, 0, at], grad.at[k, source, at],
                    s_slot[k].at[ch, 0], r_slot[k].at[ch, source], (dp, own),
                )

                @pl.when(jnp.logical_not(jnp.logical_and(chip == own, source == chip)))
                def _():
                    c.wait_recv()

        g = grad[k].reshape(chips * piece, cols)
        w = weights[k].reshape(chips * piece, rank)
        value = lax.dot_general(g, w, (((0,), (0,)), ((), ())), preferred_element_type=F32)
        value = value.T.astype(BF16)
        for t in range(chips):
            for s in range(2):
                at = (2 * t + s) * rank_rows
                part[s, k, t] = value[at : at + rank_rows]
        c = remote(part.at[other, k], part_in.at[k], s_part.at[k], r_part.at[k], partner)
        c.start()
        parts[k] = c
        sends.append(c)

    def share(k):
        parts[k].wait_recv()
        for t in range(chips):
            pair_sum[k, t] = (part[core, k, t].astype(F32) + part_in[k, t].astype(F32)).astype(BF16)
        for d in range(1, chips):
            to = lax.rem(chip + d, chips)
            c = remote(
                pair_sum.at[k, to], share_in.at[k, d - 1],
                s_share.at[k, d], r_share.at[k, d], at_chip(to),
            )
            c.start()
            shares[k, d] = c
            sends.append(c)

    def step(k):
        for d in range(1, chips):
            shares[k, d].wait_recv()
        value = pair_sum[k, chip].astype(F32)
        for d in range(1, chips):
            value = value + share_in[k, d - 1].astype(F32)
        first = beta_one * old[0, k] + (1.0 - beta_one) * value
        second = beta_two * old[1, k] + (1.0 - beta_two) * value * value
        moments[0, k] = first
        moments[1, k] = second
        taken = first / correct_one / (jnp.sqrt(second / correct_two) + adam_eps)
        mixed[k, dp, 0] = taken.astype(BF16)
        mixed[k, dp, 1] = value.astype(BF16)
        for d in range(1, chips):
            to = lax.rem(chip + d, chips)
            c = remote(mixed.at[k, dp], mixed.at[k, dp], s_mix.at[k, d], r_mix.at[k, d], at_chip(to))
            c.start()
            mix[k, d] = c
            sends.append(c)
        c = remote(mixed.at[k, dp], mixed.at[k, dp], s_mixf.at[k, 0], r_mixf.at[k, 0], partner)
        c.start()
        forward[k, 0] = c
        sends.append(c)
        for i, target in ((0, m1_out), (1, m2_out)):
            c = pltpu.make_async_copy(moments.at[i, k], target.at[k], moment_sem.at[i, k])
            c.start()
            copies.append(c)

    def mix_forward(k):
        for d in range(1, chips):
            mix[k, d].wait_recv()
            at = 2 * lax.rem(chip + chips - d, chips) + core
            c = remote(mixed.at[k, at], mixed.at[k, at], s_mixf.at[k, d], r_mixf.at[k, d], partner)
            c.start()
            forward[k, d] = c
            sends.append(c)

    def combine(k):
        for d in range(chips):
            forward[k, d].wait_recv()
        taken = mixed[k, :, 0].reshape(rank, cols).astype(F32)
        value = mixed[k, :, 1].reshape(rank, cols).astype(F32)
        grad_sum = jnp.sum(value * value, axis=0, keepdims=True)
        step_sum = jnp.sum(taken * taken, axis=0, keepdims=True)
        scale[k] = jnp.sqrt(step_sum) / (jnp.sqrt(grad_sum) + norm_eps)
        combined[k] = (taken - scale[k] * value).astype(BF16)

    def spread(k, ch):
        count = BACK_CHUNKS
        size = piece // count
        at = rows(ch, count)
        w = weights[k, :, at].reshape(chips * size, rank)
        value = jnp.dot(w, combined[k], preferred_element_type=F32)
        g = grad[k, :, at].reshape(chips * size, cols).astype(F32)
        value = (value + scale[k] * g).astype(BF16)
        for t in range(chips):
            update[k, t, at] = value[t * size : (t + 1) * size]
        for d in range(1, chips):
            to = lax.rem(chip + d, chips)
            c = remote(
                update.at[k, to, at], row_in.at[k, chip, at],
                s_back[k].at[ch, d], r_back[k].at[ch, d], at_chip(to),
            )
            c.start()
            back[k, ch, d] = c
            sends.append(c)
        row_in[k, chip, at] = update[k, chip, at]

    def go_home(k, ch):
        at = rows(ch, BACK_CHUNKS)
        for d in range(1, chips):
            back[k, ch, d].wait_recv()
        for dz in range(m - 1):
            to = plane_at(dz)
            c = remote(
                row_in.at[k, to, at], plane_in[k][ch].at[own],
                s_home[k].at[ch, dz], r_home[k].at[ch, dz], (dp, to),
            )
            c.start()
            home[k, ch, dz] = c
            sends.append(c)
        plane_in[k][ch][own] = row_in[k, own, at]

    def pick(k, ch):
        count = BACK_CHUNKS
        at = rows(ch, count)
        for dz in range(m - 1):
            home[k, ch, dz].wait_recv()
        lo, hi = back_ranges[k]
        for p in range(lo, hi):
            who = jnp.int32(0)
            slot = jnp.int32(0)
            for j in range(mats):
                who = jnp.where(position[j] == p, owner[j], who)
                slot = jnp.where(position[j] == p, within[j], slot)
            value = plane_in[0][ch][who]
            for i in range(1, k + 1):
                value = jnp.where(slot == i, plane_in[i][ch][who], value)
            picked[p, at] = value
        for d in reach:
            to = away(d)
            c = remote(
                picked.at[lo:hi, at], gathered.at[lo:hi, core, chip, at],
                s_out[k].at[ch, d], r_out[k].at[ch, d], at_chip(to),
            )
            c.start()
            gather[k, ch, d] = c
        c = remote(
            picked.at[lo:hi, at], gathered.at[lo:hi, core, chip, at],
            s_outf[k].at[ch, 0], r_outf[k].at[ch, 0], partner,
        )
        c.start()
        handed[k, ch, 0] = c
        c = pltpu.make_async_copy(
            picked.at[lo:hi, at], gathered.at[lo:hi, core, chip, at], local_sem[k].at[ch]
        )
        c.start()
        copies.append(c)

    def pass_on(k, ch):
        at = rows(ch, BACK_CHUNKS)
        half = piece // BACK_CHUNKS // 2
        lo, hi = back_ranges[k]
        for d in reach:
            gather[k, ch, d].wait_recv()
            source = from_(d)
            if square:
                part_at = pl.ds(ch * 2 * half + (half if d == 2 else 0), half)
                block = gathered.at[lo:hi, core, source, part_at]
                c = remote(
                    block, block, s_diag[k].at[ch, d], r_diag[k].at[ch, d], at_chip(away(3 - d))
                )
                c.start()
                gather[k, ch, 2 + d] = c
            block = gathered.at[lo:hi, core, source, at]
            c = remote(block, block, s_outf[k].at[ch, d], r_outf[k].at[ch, d], partner)
            c.start()
            handed[k, ch, d] = c

    def hand(k, ch):
        if not square:
            return
        at = rows(ch, BACK_CHUNKS)
        lo, hi = back_ranges[k]
        for d in reach:
            gather[k, ch, 2 + d].wait_recv()
        block = gathered.at[lo:hi, core, 3 - chip, at]
        c = remote(block, block, s_outf[k].at[ch, 3], r_outf[k].at[ch, 3], partner)
        c.start()
        handed[k, ch, 3] = c

    marked = [0]

    def drain():
        count = marked[0]
        for c in sends[:count]:
            c.wait_send()
        del sends[:count]
        marked[0] = len(sends)

    for name, k, ch in ORDER:
        if name == "o":
            for i in range(OUT_CHUNKS[k]):
                out_step(k, i)
        elif name == "p":
            if k == 0:
                load_proj.wait()
                for c in load_old:
                    c.wait()
            project(k)
        elif name == "s":
            share(k)
        elif name == "a":
            step(k)
        elif name == "f":
            mix_forward(k)
        elif name == "c":
            combine(k)
        elif name == "u":
            spread(k, ch)
        elif name == "h":
            go_home(k, ch)
        elif name == "k":
            pick(k, ch)
        elif name == "g":
            pass_on(k, ch)
        elif name == "d":
            hand(k, ch)
        elif name == "w":
            drain()

    for c in handed.values():
        c.wait_recv()
    sends += list(gather.values()) + list(handed.values())
    for c in copies:
        c.wait()
    for c in sends:
        c.wait_send()
    for sent, c in guarded:

        @pl.when(sent)
        def _():
            c.wait_send()


def out_bounds(mats, cap, owners):
    ends = [min(mats - cap + 1, owners)]
    for k in range(1, cap):
        ends.append(min(mats - cap + 1 + k, owners * (k + 1)))
    ends[-1] = mats
    return ends


def back_bounds(mats, cap):
    return [-(-mats * (k + 1) // cap) for k in range(cap)]


def steps(text):
    listed = []
    for token in text:
        if len(token) == 3:
            listed.append((token[0], int(token[1]), int(token[2])))
        elif token[0] in "uhkgd":
            listed += [(token[0], int(token[1]), ch) for ch in range(BACK_CHUNKS)]
        else:
            listed.append((token[0], int(token[1]), 0))
    return listed


ORDER = steps((
    "o0", "o1", "o2", "w0", "p0", "s0", "p1", "s1", "a0", "p2", "a1", "s2", "f0", "c0", "u0", "w0", "f1", "a2",
    "c1", "u1", "h0", "f2", "c2", "u2", "h1", "w0", "k0", "g0", "h2", "k1", "d0", "g1", "w0", "k2", "d1", "g2", "d2",
))


def settle(plan, gathered, first, second, out, first_out, second_out, sem):
    mats = out.shape[0]
    _, _, position = places_of(plan, mats)
    copies = []
    for j in range(mats):
        copies.append(pltpu.make_async_copy(gathered.at[position[j]], out.at[j], sem.at[j]))
    copies.append(pltpu.make_async_copy(first, first_out, sem.at[mats]))
    copies.append(pltpu.make_async_copy(second, second_out, sem.at[mats + 1]))
    for c in copies:
        c.start()
    for c in copies:
        c.wait()


def local(grads, proj, moment1, moment2, plan):
    n = lax.axis_size("dp")
    m = lax.axis_size("own")
    chips = n // 2
    mats, own_rows, cols = grads.shape[1:]
    cap, held_rows, rank = proj.shape[1:]
    rank_rows = moment1.shape[2]
    piece = held_rows // chips
    g = grads.reshape(mats, 2, chips, piece, cols)
    w = proj.reshape(cap, chips, piece, rank)
    hbm = pl.BlockSpec(memory_space=pltpu.HBM)
    smem = pl.BlockSpec(memory_space=pltpu.SMEM)
    anywhere = pl.BlockSpec(memory_space=pl.ANY)
    dma = pltpu.SemaphoreType.DMA
    share = (cap, rank_rows, cols)
    oc, bc = OUT_CHUNKS, (BACK_CHUNKS,) * cap

    def per_slot(counts, *shape):
        return [dma((c,) + shape) for c in counts]

    outs = (
        jax.ShapeDtypeStruct(g.shape, BF16),
        jax.ShapeDtypeStruct(share, F32),
        jax.ShapeDtypeStruct(share, F32),
    )
    gathered, first, second = pl.pallas_call(
        functools.partial(kernel, n, m),
        out_shape=outs,
        in_specs=[smem, hbm, hbm, hbm, hbm],
        out_specs=(anywhere, anywhere, anywhere),
        scratch_shapes=[
            pltpu.VMEM((mats, chips, piece, cols), BF16),
            pltpu.VMEM((mats, chips, piece, cols), BF16),
            pltpu.VMEM((mats, chips, piece, cols), BF16),
            pltpu.VMEM((mats, chips, piece, cols), BF16),
            pltpu.VMEM((chips, mats, piece, cols), BF16),
            pltpu.VMEM((chips - 1, mats, piece, cols), BF16),
            pltpu.VMEM((mats, piece, cols), BF16),
            pltpu.VMEM((cap, m, piece, cols), BF16),
            pltpu.VMEM((cap, chips, piece, cols), BF16),
            pltpu.VMEM((cap, chips, piece, rank), BF16),
            pltpu.VMEM((2, cap, chips, rank_rows, cols), BF16),
            pltpu.VMEM((cap, chips, rank_rows, cols), BF16),
            pltpu.VMEM((cap, chips, rank_rows, cols), BF16),
            pltpu.VMEM((cap, chips - 1, rank_rows, cols), BF16),
            pltpu.VMEM((cap, n, 2, rank_rows, cols), BF16),
            pltpu.VMEM((cap, chips, piece, cols), BF16),
            pltpu.VMEM((cap, chips, piece, cols), BF16),
            [[pltpu.VMEM((m, piece // BACK_CHUNKS, cols), BF16)] * BACK_CHUNKS] * cap,
            pltpu.VMEM((mats, piece, cols), BF16),
            pltpu.VMEM((2, cap, rank_rows, cols), F32),
            pltpu.VMEM((2, cap, rank_rows, cols), F32),
            dma((5,)), dma((2, cap)), per_slot(bc),
            per_slot(oc), per_slot(oc),
            per_slot(oc, chips), per_slot(oc, chips),
            per_slot(oc, m), per_slot(oc, chips),
            dma((cap,)), dma((cap,)),
            dma((cap, chips)), dma((cap, chips)),
            dma((cap, chips)), dma((cap, chips)),
            dma((cap, chips)), dma((cap, chips)),
            per_slot(bc, chips), per_slot(bc, chips),
            per_slot(bc, m), per_slot(bc, m),
            per_slot(bc, chips), per_slot(bc, chips),
            per_slot(bc, chips), per_slot(bc, chips),
            per_slot(bc, chips), per_slot(bc, chips),
        ],
        compiler_params=pltpu.CompilerParams(
            collective_id=0, has_side_effects=True, vmem_limit_bytes=44 * 2**20
        ),
    )(*(pltpu.with_memory_space_constraint(x, pltpu.HBM) for x in (plan, g, w, moment1[0], moment2[0])))
    update, first, second = pl.pallas_call(
        settle,
        out_shape=outs,
        in_specs=[smem, anywhere, anywhere, anywhere],
        out_specs=(anywhere, anywhere, anywhere),
        scratch_shapes=[dma((mats + 2,))],
        compiler_params=pltpu.CompilerParams(vmem_limit_bytes=2**20),
    )(pltpu.with_memory_space_constraint(plan, pltpu.HBM), gathered, first, second)
    return (update.reshape(mats, own_rows, cols), first[None], second[None])


def solution(mesh):
    return jax.shard_map(
        local,
        mesh=mesh,
        in_specs=(
            P("dp", None, "own", None),
            P("own", None, "dp", None),
            P("own", None, "dp", None),
            P("own", None, "dp", None),
            P(),
        ),
        out_specs=(P(None, "own", None), P("own", None, "dp", None), P("own", None, "dp", None)),
        check_vma=False,
    )
```

```python
import functools
import jax
import jax.numpy as jnp
from jax import lax
from jax.experimental import pallas as pl
from jax.experimental.pallas import tpu as pltpu
from jax.sharding import PartitionSpec as P

beta_one = 0.9
beta_two = 0.999
adam_eps = 1e-08
norm_eps = 1e-06
correct_one = 1.0 - 0.9**10
correct_two = 1.0 - 0.999**10

OUT_CHUNKS = (4, 2, 2)
AHEAD = 3
LAG = 2
BACK_CHUNKS = 2
F32 = jnp.float32
BF16 = jnp.bfloat16
MESH = pl.DeviceIdType.MESH


def places_of(plan, mats):
    owner = [plan[j] for j in range(mats)]
    within = []
    for j in range(mats):
        before = jnp.int32(0)
        for i in range(j):
            before = before + jnp.where(owner[i] == owner[j], 1, 0)
        within.append(before)
    position = []
    for j in range(mats):
        ahead = jnp.int32(0)
        for i in range(mats):
            if i < j:
                ahead = ahead + jnp.where(within[i] <= within[j], 1, 0)
            elif i > j:
                ahead = ahead + jnp.where(within[i] < within[j], 1, 0)
        position.append(ahead)
    return owner, within, position


def kernel(
    n, m, plan, grads, proj, m1_ref, m2_ref, gathered, m1_out, m2_out,
    held_core, held_other, pair_out, pair_in, half_sum, chip_in, mid_in, total, slot_out, grad, weights,
    part, part_in, pair_sum, share_in, mixed, update, row_in, plane_in, picked,
    old, moments,
    load_sem, moment_sem, local_sem,
    s_pair, r_pair, s_chip, r_chip, s_slot, r_slot,
    s_part, r_part, s_share, r_share, s_mix, r_mix, s_mixf, r_mixf,
    s_back, r_back, s_home, r_home, s_out, r_out, s_diag, r_diag, s_outf, r_outf,
):
    mats = grads.shape[0]
    chips = n // 2
    piece = grads.shape[3]
    cap = m1_ref.shape[0]
    rank_rows = m1_ref.shape[1]
    cols = m1_ref.shape[2]
    rank = n * rank_rows
    dp = lax.axis_index("dp")
    own = lax.axis_index("own")
    core = lax.rem(dp, 2)
    chip = lax.div(dp, 2)
    other = 1 - core
    partner = (2 * chip + other, own)
    out_ends = out_bounds(mats, cap, m)
    back_ends = back_bounds(mats, cap)
    out_ranges = list(zip([0] + out_ends[:-1], out_ends))
    back_ranges = list(zip([0] + back_ends[:-1], back_ends))

    def at_chip(which):
        return (2 * which + core, own)

    square = chips == 4
    reach = (1, 2) if square else tuple(range(1, chips))

    def away(d):
        if not square:
            return lax.rem(chip + d, chips)
        return chip + 1 - 2 * lax.rem(chip, 2) if d == 1 else lax.rem(chip + 2, chips)

    def from_(d):
        return away(d) if square else lax.rem(chip + chips - d, chips)

    def remote(src, dst, send, recv, device):
        return pltpu.make_async_remote_copy(
            src_ref=src, dst_ref=dst, send_sem=send, recv_sem=recv,
            device_id=device, device_id_type=MESH,
        )

    def rows(ch, count):
        size = piece // count
        return pl.ds(ch * size, size)

    barrier = pltpu.get_barrier_semaphore()

    def plane_at(i):
        h = m // 2
        half = lax.div(own, h)
        if i < m - h:
            return (1 - half) * h + lax.rem(own + i, h)
        return half * h + lax.rem(own + i - h + 1, h)

    greeted = [(dp, lax.rem(own + d, m)) for d in range(1, m)]
    greeted += [at_chip(lax.rem(chip + d, chips)) for d in range(1, chips)] + [partner]
    for device in greeted:
        pl.semaphore_signal(barrier, inc=1, device_id=device, device_id_type=MESH)

    load_other = pltpu.make_async_copy(grads.at[:, other], held_other, load_sem.at[0])
    load_other.start()
    load_core = pltpu.make_async_copy(grads.at[:, core], held_core, load_sem.at[1])
    load_core.start()
    load_proj = pltpu.make_async_copy(proj, weights, load_sem.at[2])
    load_proj.start()
    load_old = [
        pltpu.make_async_copy(m1_ref, old.at[0], load_sem.at[3]),
        pltpu.make_async_copy(m2_ref, old.at[1], load_sem.at[4]),
    ]
    for c in load_old:
        c.start()

    owner, within, position = places_of(plan, mats)
    order = []
    for p in range(mats):
        index = jnp.int32(0)
        for j in range(mats):
            index = jnp.where(position[j] == p, j, index)
        order.append(index)

    def occupant(plane, k):
        at = jnp.int32(0)
        valid = jnp.int32(0)
        for j in range(mats):
            here = jnp.logical_and(owner[j] == plane, within[j] == k)
            at = jnp.where(here, position[j], at)
            valid = jnp.where(here, 1, valid)
        return at, valid.astype(F32)

    sends = []
    guarded = []
    out_units = [(g, ch) for g in range(cap) for ch in range(OUT_CHUNKS[g])]

    load_other.wait()
    pair = {}
    first_unit = True
    for g, ch in out_units:
        at = rows(ch, OUT_CHUNKS[g])
        lo, hi = out_ranges[g]
        for p in range(lo, hi):
            pair_out[p, :, at] = held_other[order[p], :, at]
        if first_unit:
            pl.semaphore_wait(barrier, len(greeted))
            first_unit = False
        c = remote(
            pair_out.at[lo:hi, :, at], pair_in.at[lo:hi, :, at],
            s_pair[g].at[ch], r_pair[g].at[ch], partner,
        )
        c.start()
        pair[g, ch] = c
    sends += list(pair.values())

    load_core.wait()
    over = {}

    def halves(g, ch):
        size = piece // OUT_CHUNKS[g]
        return pl.ds(ch * size, size // 2), pl.ds(ch * size + size // 2, size // 2)

    def send_over(g, ch, i, src, dst, device):
        c = remote(src, dst, s_chip[g].at[ch, i], r_chip[g].at[ch, i], device)
        c.start()
        over[g, ch, i] = c
        sends.append(c)

    def pair_step(g, ch):
        at = rows(ch, OUT_CHUNKS[g])
        lo, hi = out_ranges[g]
        pair[g, ch].wait_recv()
        for p in range(lo, hi):

            @pl.loop(0, chips)
            def _(t):
                half_sum[t, p, at] = (
                    held_core[order[p], t, at].astype(F32) + pair_in[p, t, at].astype(F32)
                ).astype(BF16)

        if square:
            a, b = halves(g, ch)
            x, y, diagonal = away(1), away(2), 3 - chip
            for i, to, half, which in ((0, x, a, diagonal), (1, y, b, diagonal)):
                send_over(
                    g, ch, i, half_sum.at[which, lo:hi, half], mid_in.at[i, lo:hi, half], at_chip(to)
                )
            for i, to, half in ((2, x, a), (3, y, b)):
                send_over(
                    g, ch, i, half_sum.at[to, lo:hi, half], chip_in.at[i - 2, lo:hi, half], at_chip(to)
                )
        else:
            for d in range(1, chips):
                to = away(d)
                send_over(
                    g, ch, d, half_sum.at[to, lo:hi, at], chip_in.at[d - 1, lo:hi, at], at_chip(to)
                )

    def relay_step(g, ch):
        if not square:
            return
        lo, hi = out_ranges[g]
        a, b = halves(g, ch)
        for i, to, half in ((0, away(2), a), (1, away(1), b)):
            over[g, ch, i].wait_recv()
            for p in range(lo, hi):
                half_sum[to, p, half] = (
                    half_sum[to, p, half].astype(F32) + mid_in[i, p, half].astype(F32)
                ).astype(BF16)
            send_over(
                g, ch, 4 + i, half_sum.at[to, lo:hi, half], chip_in.at[1 - i, lo:hi, half], at_chip(to)
            )

    def out_step(g, ch):
        count = OUT_CHUNKS[g]
        at = rows(ch, count)
        lo, hi = out_ranges[g]
        for i in (2, 3, 4, 5) if square else range(1, chips):
            over[g, ch, i].wait_recv()
        for p in range(lo, hi):
            acc = half_sum[chip, p, at].astype(F32)
            for d in reach:
                acc = acc + chip_in[d - 1, p, at].astype(F32)
            total[p, at] = acc.astype(BF16)
        for i in range(m):
            z = plane_at(i)
            index, valid = occupant(z, g)
            slot_out[g, z, at] = (total[index, at].astype(F32) * valid).astype(BF16)
            c = remote(
                slot_out.at[g, z, at], grad.at[g, chip, at],
                s_slot[g].at[ch, i], r_slot[g].at[ch, chip], (2 * own + core, z),
            )
            mine = jnp.logical_and(own == z, chip == own)

            @pl.when(jnp.logical_not(mine))
            def _():
                c.start()

            @pl.when(mine)
            def _():
                grad[g, chip, at] = slot_out[g, z, at]

            guarded.append((jnp.logical_not(mine), c))

    parts = {}
    shares = {}
    combined = {}
    scale = {}
    mix = {}
    forward = {}
    back = {}
    home = {}
    gather = {}
    handed = {}
    copies = []

    def project(k):
        count = OUT_CHUNKS[k]
        for ch in range(count):
            for source in range(chips):
                at = rows(ch, count)
                c = remote(
                    slot_out.at[k, 0, at], grad.at[k, source, at],
                    s_slot[k].at[ch, 0], r_slot[k].at[ch, source], (dp, own),
                )

                @pl.when(jnp.logical_not(jnp.logical_and(chip == own, source == chip)))
                def _():
                    c.wait_recv()

        g = grad[k].reshape(chips * piece, cols)
        w = weights[k].reshape(chips * piece, rank)
        value = lax.dot_general(g, w, (((0,), (0,)), ((), ())), preferred_element_type=F32)
        value = value.T.astype(BF16)
        for t in range(chips):
            for s in range(2):
                at = (2 * t + s) * rank_rows
                part[s, k, t] = value[at : at + rank_rows]
        c = remote(part.at[other, k], part_in.at[k], s_part.at[k], r_part.at[k], partner)
        c.start()
        parts[k] = c
        sends.append(c)

    def share(k):
        parts[k].wait_recv()
        for t in range(chips):
            pair_sum[k, t] = (part[core, k, t].astype(F32) + part_in[k, t].astype(F32)).astype(BF16)
        for d in range(1, chips):
            to = lax.rem(chip + d, chips)
            c = remote(
                pair_sum.at[k, to], share_in.at[k, d - 1],
                s_share.at[k, d], r_share.at[k, d], at_chip(to),
            )
            c.start()
            shares[k, d] = c
            sends.append(c)

    def step(k):
        for d in range(1, chips):
            shares[k, d].wait_recv()
        value = pair_sum[k, chip].astype(F32)
        for d in range(1, chips):
            value = value + share_in[k, d - 1].astype(F32)
        first = beta_one * old[0, k] + (1.0 - beta_one) * value
        second = beta_two * old[1, k] + (1.0 - beta_two) * value * value
        moments[0, k] = first
        moments[1, k] = second
        taken = first / correct_one / (jnp.sqrt(second / correct_two) + adam_eps)
        mixed[k, dp, 0] = taken.astype(BF16)
        mixed[k, dp, 1] = value.astype(BF16)
        for d in range(1, chips):
            to = lax.rem(chip + d, chips)
            c = remote(mixed.at[k, dp], mixed.at[k, dp], s_mix.at[k, d], r_mix.at[k, d], at_chip(to))
            c.start()
            mix[k, d] = c
            sends.append(c)
        c = remote(mixed.at[k, dp], mixed.at[k, dp], s_mixf.at[k, 0], r_mixf.at[k, 0], partner)
        c.start()
        forward[k, 0] = c
        sends.append(c)
        for i, target in ((0, m1_out), (1, m2_out)):
            c = pltpu.make_async_copy(moments.at[i, k], target.at[k], moment_sem.at[i, k])
            c.start()
            copies.append(c)

    def mix_forward(k):
        for d in range(1, chips):
            mix[k, d].wait_recv()
            at = 2 * lax.rem(chip + chips - d, chips) + core
            c = remote(mixed.at[k, at], mixed.at[k, at], s_mixf.at[k, d], r_mixf.at[k, d], partner)
            c.start()
            forward[k, d] = c
            sends.append(c)

    def combine(k):
        for d in range(chips):
            forward[k, d].wait_recv()
        taken = mixed[k, :, 0].reshape(rank, cols).astype(F32)
        value = mixed[k, :, 1].reshape(rank, cols).astype(F32)
        grad_sum = jnp.sum(value * value, axis=0, keepdims=True)
        step_sum = jnp.sum(taken * taken, axis=0, keepdims=True)
        scale[k] = jnp.sqrt(step_sum) / (jnp.sqrt(grad_sum) + norm_eps)
        combined[k] = (taken - scale[k] * value).astype(BF16)

    def spread(k, ch):
        count = BACK_CHUNKS
        size = piece // count
        at = rows(ch, count)
        w = weights[k, :, at].reshape(chips * size, rank)
        value = jnp.dot(w, combined[k], preferred_element_type=F32)
        g = grad[k, :, at].reshape(chips * size, cols).astype(F32)
        value = (value + scale[k] * g).astype(BF16)
        for t in range(chips):
            update[k, t, at] = value[t * size : (t + 1) * size]
        for d in range(1, chips):
            to = lax.rem(chip + d, chips)
            c = remote(
                update.at[k, to, at], row_in.at[k, chip, at],
                s_back[k].at[ch, d], r_back[k].at[ch, d], at_chip(to),
            )
            c.start()
            back[k, ch, d] = c
            sends.append(c)
        row_in[k, chip, at] = update[k, chip, at]

    def go_home(k, ch):
        at = rows(ch, BACK_CHUNKS)
        for d in range(1, chips):
            back[k, ch, d].wait_recv()
        for dz in range(m - 1):
            to = plane_at(dz)
            c = remote(
                row_in.at[k, to, at], plane_in[k][ch].at[own],
                s_home[k].at[ch, dz], r_home[k].at[ch, dz], (dp, to),
            )
            c.start()
            home[k, ch, dz] = c
            sends.append(c)
        plane_in[k][ch][own] = row_in[k, own, at]

    def pick(k, ch):
        count = BACK_CHUNKS
        at = rows(ch, count)
        for dz in range(m - 1):
            home[k, ch, dz].wait_recv()
        lo, hi = back_ranges[k]
        for p in range(lo, hi):
            who = jnp.int32(0)
            slot = jnp.int32(0)
            for j in range(mats):
                who = jnp.where(position[j] == p, owner[j], who)
                slot = jnp.where(position[j] == p, within[j], slot)
            value = plane_in[0][ch][who]
            for i in range(1, k + 1):
                value = jnp.where(slot == i, plane_in[i][ch][who], value)
            picked[p, at] = value
        for d in reach:
            to = away(d)
            c = remote(
                picked.at[lo:hi, at], gathered.at[lo:hi, core, chip, at],
                s_out[k].at[ch, d], r_out[k].at[ch, d], at_chip(to),
            )
            c.start()
            gather[k, ch, d] = c
        c = remote(
            picked.at[lo:hi, at], gathered.at[lo:hi, core, chip, at],
            s_outf[k].at[ch, 0], r_outf[k].at[ch, 0], partner,
        )
        c.start()
        handed[k, ch, 0] = c
        c = pltpu.make_async_copy(
            picked.at[lo:hi, at], gathered.at[lo:hi, core, chip, at], local_sem[k].at[ch]
        )
        c.start()
        copies.append(c)

    def pass_on(k, ch):
        at = rows(ch, BACK_CHUNKS)
        half = piece // BACK_CHUNKS // 2
        lo, hi = back_ranges[k]
        for d in reach:
            gather[k, ch, d].wait_recv()
            source = from_(d)
            if square:
                part_at = pl.ds(ch * 2 * half + (half if d == 2 else 0), half)
                block = gathered.at[lo:hi, core, source, part_at]
                c = remote(
                    block, block, s_diag[k].at[ch, d], r_diag[k].at[ch, d], at_chip(away(3 - d))
                )
                c.start()
                gather[k, ch, 2 + d] = c
            block = gathered.at[lo:hi, core, source, at]
            c = remote(block, block, s_outf[k].at[ch, d], r_outf[k].at[ch, d], partner)
            c.start()
            handed[k, ch, d] = c

    def hand(k, ch):
        if not square:
            return
        at = rows(ch, BACK_CHUNKS)
        lo, hi = back_ranges[k]
        for d in reach:
            gather[k, ch, 2 + d].wait_recv()
        block = gathered.at[lo:hi, core, 3 - chip, at]
        c = remote(block, block, s_outf[k].at[ch, 3], r_outf[k].at[ch, 3], partner)
        c.start()
        handed[k, ch, 3] = c

    marked = [0]

    def drain():
        count = marked[0]
        for c in sends[:count]:
            c.wait_send()
        del sends[:count]
        marked[0] = len(sends)

    units = len(out_units)
    for i in range(units + AHEAD + LAG):
        if i < units:
            pair_step(*out_units[i])
        if 0 <= i - AHEAD < units:
            relay_step(*out_units[i - AHEAD])
        if 0 <= i - AHEAD - LAG:
            out_step(*out_units[i - AHEAD - LAG])

    for name, k, ch in ORDER:
        if name == "p":
            if k == 0:
                load_proj.wait()
                for c in load_old:
                    c.wait()
            project(k)
        elif name == "s":
            share(k)
        elif name == "a":
            step(k)
        elif name == "f":
            mix_forward(k)
        elif name == "c":
            combine(k)
        elif name == "u":
            spread(k, ch)
        elif name == "h":
            go_home(k, ch)
        elif name == "k":
            pick(k, ch)
        elif name == "g":
            pass_on(k, ch)
        elif name == "d":
            hand(k, ch)
        elif name == "w":
            drain()

    for c in handed.values():
        c.wait_recv()
    sends += list(gather.values()) + list(handed.values())
    for c in copies:
        c.wait()
    for c in sends:
        c.wait_send()
    for sent, c in guarded:

        @pl.when(sent)
        def _():
            c.wait_send()


def out_bounds(mats, cap, owners):
    ends = [min(mats - cap + 1, owners)]
    for k in range(1, cap):
        ends.append(min(mats - cap + 1 + k, owners * (k + 1)))
    ends[-1] = mats
    return ends


def back_bounds(mats, cap):
    return [-(-mats * (k + 1) // cap) for k in range(cap)]


def steps(text):
    listed = []
    for token in text:
        if len(token) == 3:
            listed.append((token[0], int(token[1]), int(token[2])))
        elif token[0] in "uhkgd":
            listed += [(token[0], int(token[1]), ch) for ch in range(BACK_CHUNKS)]
        else:
            listed.append((token[0], int(token[1]), 0))
    return listed


ORDER = steps((
    "w0", "p0", "s0", "p1", "s1", "a0", "p2", "a1", "s2", "f0", "c0", "u0", "w0", "f1", "a2",
    "c1", "u1", "h0", "f2", "c2", "u2", "h1", "w0", "k0", "g0", "h2", "k1", "d0", "g1", "w0", "k2", "d1", "g2", "d2",
))


def settle(plan, gathered, first, second, out, first_out, second_out, sem):
    mats = out.shape[0]
    _, _, position = places_of(plan, mats)
    copies = []
    for j in range(mats):
        copies.append(pltpu.make_async_copy(gathered.at[position[j]], out.at[j], sem.at[j]))
    copies.append(pltpu.make_async_copy(first, first_out, sem.at[mats]))
    copies.append(pltpu.make_async_copy(second, second_out, sem.at[mats + 1]))
    for c in copies:
        c.start()
    for c in copies:
        c.wait()


def local(grads, proj, moment1, moment2, plan):
    n = lax.axis_size("dp")
    m = lax.axis_size("own")
    chips = n // 2
    mats, own_rows, cols = grads.shape[1:]
    cap, held_rows, rank = proj.shape[1:]
    rank_rows = moment1.shape[2]
    piece = held_rows // chips
    g = grads.reshape(mats, 2, chips, piece, cols)
    w = proj.reshape(cap, chips, piece, rank)
    hbm = pl.BlockSpec(memory_space=pltpu.HBM)
    smem = pl.BlockSpec(memory_space=pltpu.SMEM)
    anywhere = pl.BlockSpec(memory_space=pl.ANY)
    dma = pltpu.SemaphoreType.DMA
    share = (cap, rank_rows, cols)
    oc, bc = OUT_CHUNKS, (BACK_CHUNKS,) * cap

    def per_slot(counts, *shape):
        return [dma((c,) + shape) for c in counts]

    outs = (
        jax.ShapeDtypeStruct(g.shape, BF16),
        jax.ShapeDtypeStruct(share, F32),
        jax.ShapeDtypeStruct(share, F32),
    )
    gathered, first, second = pl.pallas_call(
        functools.partial(kernel, n, m),
        out_shape=outs,
        in_specs=[smem, hbm, hbm, hbm, hbm],
        out_specs=(anywhere, anywhere, anywhere),
        scratch_shapes=[
            pltpu.VMEM((mats, chips, piece, cols), BF16),
            pltpu.VMEM((mats, chips, piece, cols), BF16),
            pltpu.VMEM((mats, chips, piece, cols), BF16),
            pltpu.VMEM((mats, chips, piece, cols), BF16),
            pltpu.VMEM((chips, mats, piece, cols), BF16),
            pltpu.VMEM((chips - 1, mats, piece, cols), BF16),
            pltpu.VMEM((2, mats, piece, cols), BF16),
            pltpu.VMEM((mats, piece, cols), BF16),
            pltpu.VMEM((cap, m, piece, cols), BF16),
            pltpu.VMEM((cap, chips, piece, cols), BF16),
            pltpu.VMEM((cap, chips, piece, rank), BF16),
            pltpu.VMEM((2, cap, chips, rank_rows, cols), BF16),
            pltpu.VMEM((cap, chips, rank_rows, cols), BF16),
            pltpu.VMEM((cap, chips, rank_rows, cols), BF16),
            pltpu.VMEM((cap, chips - 1, rank_rows, cols), BF16),
            pltpu.VMEM((cap, n, 2, rank_rows, cols), BF16),
            pltpu.VMEM((cap, chips, piece, cols), BF16),
            pltpu.VMEM((cap, chips, piece, cols), BF16),
            [[pltpu.VMEM((m, piece // BACK_CHUNKS, cols), BF16)] * BACK_CHUNKS] * cap,
            pltpu.VMEM((mats, piece, cols), BF16),
            pltpu.VMEM((2, cap, rank_rows, cols), F32),
            pltpu.VMEM((2, cap, rank_rows, cols), F32),
            dma((5,)), dma((2, cap)), per_slot(bc),
            per_slot(oc), per_slot(oc),
            per_slot(oc, chips + 2), per_slot(oc, chips + 2),
            per_slot(oc, m), per_slot(oc, chips),
            dma((cap,)), dma((cap,)),
            dma((cap, chips)), dma((cap, chips)),
            dma((cap, chips)), dma((cap, chips)),
            dma((cap, chips)), dma((cap, chips)),
            per_slot(bc, chips), per_slot(bc, chips),
            per_slot(bc, m), per_slot(bc, m),
            per_slot(bc, chips), per_slot(bc, chips),
            per_slot(bc, chips), per_slot(bc, chips),
            per_slot(bc, chips), per_slot(bc, chips),
        ],
        compiler_params=pltpu.CompilerParams(
            collective_id=0, has_side_effects=True, vmem_limit_bytes=44 * 2**20
        ),
    )(*(pltpu.with_memory_space_constraint(x, pltpu.HBM) for x in (plan, g, w, moment1[0], moment2[0])))
    update, first, second = pl.pallas_call(
        settle,
        out_shape=outs,
        in_specs=[smem, anywhere, anywhere, anywhere],
        out_specs=(anywhere, anywhere, anywhere),
        scratch_shapes=[dma((mats + 2,))],
        compiler_params=pltpu.CompilerParams(vmem_limit_bytes=2**20),
    )(pltpu.with_memory_space_constraint(plan, pltpu.HBM), gathered, first, second)
    return (update.reshape(mats, own_rows, cols), first[None], second[None])


def solution(mesh):
    return jax.shard_map(
        local,
        mesh=mesh,
        in_specs=(
            P("dp", None, "own", None),
            P("own", None, "dp", None),
            P("own", None, "dp", None),
            P("own", None, "dp", None),
            P(),
        ),
        out_specs=(P(None, "own", None), P("own", None, "dp", None), P("own", None, "dp", None)),
        check_vma=False,
    )
```

```python
import functools
import jax
import jax.numpy as jnp
from jax import lax
from jax.experimental import pallas as pl
from jax.experimental.pallas import tpu as pltpu
from jax.sharding import PartitionSpec as P

beta_one = 0.9
beta_two = 0.999
adam_eps = 1e-08
norm_eps = 1e-06
correct_one = 1.0 - 0.9**10
correct_two = 1.0 - 0.999**10

OUT_CHUNKS = (4, 2, 2)
AHEAD = 3
LAG = 2
BACK_CHUNKS = 2
F32 = jnp.float32
BF16 = jnp.bfloat16
MESH = pl.DeviceIdType.MESH


def places_of(plan, mats):
    owner = [plan[j] for j in range(mats)]
    within = []
    for j in range(mats):
        before = jnp.int32(0)
        for i in range(j):
            before = before + jnp.where(owner[i] == owner[j], 1, 0)
        within.append(before)
    position = []
    for j in range(mats):
        ahead = jnp.int32(0)
        for i in range(mats):
            if i < j:
                ahead = ahead + jnp.where(within[i] <= within[j], 1, 0)
            elif i > j:
                ahead = ahead + jnp.where(within[i] < within[j], 1, 0)
        position.append(ahead)
    return owner, within, position


def kernel(
    n, m, plan, grads, proj, m1_ref, m2_ref, gathered, m1_out, m2_out,
    held_core, held_other, pair_out, pair_in, half_sum, chip_in, mid_in, total, slot_out, grad, weights,
    part, part_in, pair_sum, share_in, mixed, update, row_in, plane_in, picked,
    old, moments,
    load_sem, moment_sem, local_sem,
    s_pair, r_pair, s_chip, r_chip, s_slot, r_slot,
    s_part, r_part, s_share, r_share, s_mix, r_mix, s_mixf, r_mixf,
    s_back, r_back, s_home, r_home, s_out, r_out, s_diag, r_diag, s_outf, r_outf,
):
    mats = grads.shape[0]
    chips = n // 2
    piece = grads.shape[3]
    cap = m1_ref.shape[0]
    rank_rows = m1_ref.shape[1]
    cols = m1_ref.shape[2]
    rank = n * rank_rows
    dp = lax.axis_index("dp")
    own = lax.axis_index("own")
    core = lax.rem(dp, 2)
    chip = lax.div(dp, 2)
    other = 1 - core
    partner = (2 * chip + other, own)
    out_ends = out_bounds(mats, cap, m)
    back_ends = back_bounds(mats, cap)
    out_ranges = list(zip([0] + out_ends[:-1], out_ends))
    back_ranges = list(zip([0] + back_ends[:-1], back_ends))

    def at_chip(which):
        return (2 * which + core, own)

    square = chips == 4
    reach = (1, 2) if square else tuple(range(1, chips))

    def away(d):
        if not square:
            return lax.rem(chip + d, chips)
        return chip + 1 - 2 * lax.rem(chip, 2) if d == 1 else lax.rem(chip + 2, chips)

    def from_(d):
        return away(d) if square else lax.rem(chip + chips - d, chips)

    def remote(src, dst, send, recv, device):
        return pltpu.make_async_remote_copy(
            src_ref=src, dst_ref=dst, send_sem=send, recv_sem=recv,
            device_id=device, device_id_type=MESH,
        )

    def rows(ch, count):
        size = piece // count
        return pl.ds(ch * size, size)

    barrier = pltpu.get_barrier_semaphore()

    def plane_at(i):
        h = m // 2
        half = lax.div(own, h)
        if i < m - h:
            return (1 - half) * h + lax.rem(own + i, h)
        return half * h + lax.rem(own + i - h + 1, h)

    greeted = [(dp, lax.rem(own + d, m)) for d in range(1, m)]
    greeted += [at_chip(lax.rem(chip + d, chips)) for d in range(1, chips)] + [partner]
    for device in greeted:
        pl.semaphore_signal(barrier, inc=1, device_id=device, device_id_type=MESH)

    load_other = pltpu.make_async_copy(grads.at[:, other], held_other, load_sem.at[0])
    load_other.start()
    load_core = pltpu.make_async_copy(grads.at[:, core], held_core, load_sem.at[1])
    load_core.start()
    load_proj = pltpu.make_async_copy(proj, weights, load_sem.at[2])
    load_proj.start()
    load_old = [
        pltpu.make_async_copy(m1_ref, old.at[0], load_sem.at[3]),
        pltpu.make_async_copy(m2_ref, old.at[1], load_sem.at[4]),
    ]
    for c in load_old:
        c.start()

    owner, within, position = places_of(plan, mats)
    order = []
    for p in range(mats):
        index = jnp.int32(0)
        for j in range(mats):
            index = jnp.where(position[j] == p, j, index)
        order.append(index)

    def occupant(plane, k):
        at = jnp.int32(0)
        valid = jnp.int32(0)
        for j in range(mats):
            here = jnp.logical_and(owner[j] == plane, within[j] == k)
            at = jnp.where(here, position[j], at)
            valid = jnp.where(here, 1, valid)
        return at, valid.astype(F32)

    sends = []
    guarded = []
    out_units = [(g, ch) for g in range(cap) for ch in range(OUT_CHUNKS[g])]

    load_other.wait()
    pair = {}
    first_unit = True
    for g, ch in out_units:
        at = rows(ch, OUT_CHUNKS[g])
        lo, hi = out_ranges[g]
        for p in range(lo, hi):
            pair_out[p, :, at] = held_other[order[p], :, at]
        if first_unit:
            pl.semaphore_wait(barrier, len(greeted))
            first_unit = False
        c = remote(
            pair_out.at[lo:hi, :, at], pair_in.at[lo:hi, :, at],
            s_pair[g].at[ch], r_pair[g].at[ch], partner,
        )
        c.start()
        pair[g, ch] = c
    sends += list(pair.values())

    load_core.wait()
    over = {}

    def halves(g, ch):
        size = piece // OUT_CHUNKS[g]
        return pl.ds(ch * size, size // 2), pl.ds(ch * size + size // 2, size // 2)

    def send_over(g, ch, i, src, dst, device):
        c = remote(src, dst, s_chip[g].at[ch, i], r_chip[g].at[ch, i], device)
        c.start()
        over[g, ch, i] = c
        sends.append(c)

    def pair_step(g, ch):
        at = rows(ch, OUT_CHUNKS[g])
        lo, hi = out_ranges[g]
        pair[g, ch].wait_recv()
        for p in range(lo, hi):

            @pl.loop(0, chips)
            def _(t):
                half_sum[t, p, at] = (
                    held_core[order[p], t, at].astype(F32) + pair_in[p, t, at].astype(F32)
                ).astype(BF16)

        if square:
            a, b = halves(g, ch)
            x, y, diagonal = away(1), away(2), 3 - chip
            for i, to, half, which in ((0, x, a, diagonal), (1, y, b, diagonal)):
                send_over(
                    g, ch, i, half_sum.at[which, lo:hi, half], mid_in.at[i, lo:hi, half], at_chip(to)
                )
            for i, to, half in ((2, x, a), (3, y, b)):
                send_over(
                    g, ch, i, half_sum.at[to, lo:hi, half], chip_in.at[i - 2, lo:hi, half], at_chip(to)
                )
        else:
            for d in range(1, chips):
                to = away(d)
                send_over(
                    g, ch, d, half_sum.at[to, lo:hi, at], chip_in.at[d - 1, lo:hi, at], at_chip(to)
                )

    def relay_step(g, ch):
        if not square:
            return
        lo, hi = out_ranges[g]
        a, b = halves(g, ch)
        for i, to, half in ((0, away(2), a), (1, away(1), b)):
            over[g, ch, i].wait_recv()
            for p in range(lo, hi):
                half_sum[to, p, half] = (
                    half_sum[to, p, half].astype(F32) + mid_in[i, p, half].astype(F32)
                ).astype(BF16)
            send_over(
                g, ch, 4 + i, half_sum.at[to, lo:hi, half], chip_in.at[1 - i, lo:hi, half], at_chip(to)
            )

    def out_step(g, ch):
        count = OUT_CHUNKS[g]
        at = rows(ch, count)
        lo, hi = out_ranges[g]
        for i in (2, 3, 4, 5) if square else range(1, chips):
            over[g, ch, i].wait_recv()
        for p in range(lo, hi):
            acc = half_sum[chip, p, at].astype(F32)
            for d in reach:
                acc = acc + chip_in[d - 1, p, at].astype(F32)
            total[p, at] = acc.astype(BF16)
        for i in range(m):
            z = plane_at(i)
            index, valid = occupant(z, g)
            slot_out[g, z, at] = (total[index, at].astype(F32) * valid).astype(BF16)
            c = remote(
                slot_out.at[g, z, at], grad.at[g, chip, at],
                s_slot[g].at[ch, i], r_slot[g].at[ch, chip], (2 * own + core, z),
            )
            mine = jnp.logical_and(own == z, chip == own)

            @pl.when(jnp.logical_not(mine))
            def _():
                c.start()

            @pl.when(mine)
            def _():
                grad[g, chip, at] = slot_out[g, z, at]

            guarded.append((jnp.logical_not(mine), c))

    parts = {}
    shares = {}
    combined = {}
    scale = {}
    mix = {}
    forward = {}
    back = {}
    home = {}
    gather = {}
    handed = {}
    copies = []

    def project(k):
        count = OUT_CHUNKS[k]
        for ch in range(count):
            for source in range(chips):
                at = rows(ch, count)
                c = remote(
                    slot_out.at[k, 0, at], grad.at[k, source, at],
                    s_slot[k].at[ch, 0], r_slot[k].at[ch, source], (dp, own),
                )

                @pl.when(jnp.logical_not(jnp.logical_and(chip == own, source == chip)))
                def _():
                    c.wait_recv()

        g = grad[k].reshape(chips * piece, cols)
        w = weights[k].reshape(chips * piece, rank)
        value = lax.dot_general(g, w, (((0,), (0,)), ((), ())), preferred_element_type=F32)
        value = value.T.astype(BF16)
        for t in range(chips):
            for s in range(2):
                at = (2 * t + s) * rank_rows
                part[s, k, t] = value[at : at + rank_rows]
        c = remote(part.at[other, k], part_in.at[k], s_part.at[k], r_part.at[k], partner)
        c.start()
        parts[k] = c
        sends.append(c)

    def share(k):
        parts[k].wait_recv()
        for t in range(chips):
            pair_sum[k, t] = (part[core, k, t].astype(F32) + part_in[k, t].astype(F32)).astype(BF16)
        for d in range(1, chips):
            to = lax.rem(chip + d, chips)
            c = remote(
                pair_sum.at[k, to], share_in.at[k, d - 1],
                s_share.at[k, d], r_share.at[k, d], at_chip(to),
            )
            c.start()
            shares[k, d] = c
            sends.append(c)

    def step(k):
        for d in range(1, chips):
            shares[k, d].wait_recv()
        value = pair_sum[k, chip].astype(F32)
        for d in range(1, chips):
            value = value + share_in[k, d - 1].astype(F32)
        first = beta_one * old[0, k] + (1.0 - beta_one) * value
        second = beta_two * old[1, k] + (1.0 - beta_two) * value * value
        moments[0, k] = first
        moments[1, k] = second
        taken = first / correct_one / (jnp.sqrt(second / correct_two) + adam_eps)
        mixed[k, dp, 0] = taken.astype(BF16)
        mixed[k, dp, 1] = value.astype(BF16)
        for d in range(1, chips):
            to = lax.rem(chip + d, chips)
            c = remote(mixed.at[k, dp], mixed.at[k, dp], s_mix.at[k, d], r_mix.at[k, d], at_chip(to))
            c.start()
            mix[k, d] = c
            sends.append(c)
        c = remote(mixed.at[k, dp], mixed.at[k, dp], s_mixf.at[k, 0], r_mixf.at[k, 0], partner)
        c.start()
        forward[k, 0] = c
        sends.append(c)
        for i, target in ((0, m1_out), (1, m2_out)):
            c = pltpu.make_async_copy(moments.at[i, k], target.at[k], moment_sem.at[i, k])
            c.start()
            copies.append(c)

    def mix_forward(k):
        for d in range(1, chips):
            mix[k, d].wait_recv()
            at = 2 * lax.rem(chip + chips - d, chips) + core
            c = remote(mixed.at[k, at], mixed.at[k, at], s_mixf.at[k, d], r_mixf.at[k, d], partner)
            c.start()
            forward[k, d] = c
            sends.append(c)

    def combine(k):
        for d in range(chips):
            forward[k, d].wait_recv()
        taken = mixed[k, :, 0].reshape(rank, cols).astype(F32)
        value = mixed[k, :, 1].reshape(rank, cols).astype(F32)
        grad_sum = jnp.sum(value * value, axis=0, keepdims=True)
        step_sum = jnp.sum(taken * taken, axis=0, keepdims=True)
        scale[k] = jnp.sqrt(step_sum) / (jnp.sqrt(grad_sum) + norm_eps)
        combined[k] = (taken - scale[k] * value).astype(BF16)

    def spread(k, ch):
        count = BACK_CHUNKS
        size = piece // count
        at = rows(ch, count)
        w = weights[k, :, at].reshape(chips * size, rank)
        value = jnp.dot(w, combined[k], preferred_element_type=F32)
        g = grad[k, :, at].reshape(chips * size, cols).astype(F32)
        value = (value + scale[k] * g).astype(BF16)
        for t in range(chips):
            update[k, t, at] = value[t * size : (t + 1) * size]
        for d in range(1, chips):
            to = lax.rem(chip + d, chips)
            c = remote(
                update.at[k, to, at], row_in.at[k, chip, at],
                s_back[k].at[ch, d], r_back[k].at[ch, d], at_chip(to),
            )
            c.start()
            back[k, ch, d] = c
            sends.append(c)
        row_in[k, chip, at] = update[k, chip, at]

    def go_home(k, ch):
        at = rows(ch, BACK_CHUNKS)
        for d in range(1, chips):
            back[k, ch, d].wait_recv()
        for dz in range(m - 1):
            to = plane_at(dz)
            c = remote(
                row_in.at[k, to, at], plane_in[k][ch].at[own],
                s_home[k].at[ch, dz], r_home[k].at[ch, dz], (dp, to),
            )
            c.start()
            home[k, ch, dz] = c
            sends.append(c)
        plane_in[k][ch][own] = row_in[k, own, at]

    def pick(k, ch):
        count = BACK_CHUNKS
        at = rows(ch, count)
        for dz in range(m - 1):
            home[k, ch, dz].wait_recv()
        lo, hi = back_ranges[k]
        for p in range(lo, hi):
            who = jnp.int32(0)
            slot = jnp.int32(0)
            for j in range(mats):
                who = jnp.where(position[j] == p, owner[j], who)
                slot = jnp.where(position[j] == p, within[j], slot)
            value = plane_in[0][ch][who]
            for i in range(1, k + 1):
                value = jnp.where(slot == i, plane_in[i][ch][who], value)
            picked[p, at] = value
        for d in reach:
            to = away(d)
            c = remote(
                picked.at[lo:hi, at], gathered.at[lo:hi, core, chip, at],
                s_out[k].at[ch, d], r_out[k].at[ch, d], at_chip(to),
            )
            c.start()
            gather[k, ch, d] = c
        c = remote(
            picked.at[lo:hi, at], gathered.at[lo:hi, core, chip, at],
            s_outf[k].at[ch, 0], r_outf[k].at[ch, 0], partner,
        )
        c.start()
        handed[k, ch, 0] = c
        c = pltpu.make_async_copy(
            picked.at[lo:hi, at], gathered.at[lo:hi, core, chip, at], local_sem[k].at[ch]
        )
        c.start()
        copies.append(c)

    def pass_on(k, ch):
        at = rows(ch, BACK_CHUNKS)
        half = piece // BACK_CHUNKS // 2
        lo, hi = back_ranges[k]
        for d in reach:
            gather[k, ch, d].wait_recv()
            source = from_(d)
            if square:
                part_at = pl.ds(ch * 2 * half + (half if d == 2 else 0), half)
                block = gathered.at[lo:hi, core, source, part_at]
                c = remote(
                    block, block, s_diag[k].at[ch, d], r_diag[k].at[ch, d], at_chip(away(3 - d))
                )
                c.start()
                gather[k, ch, 2 + d] = c
            block = gathered.at[lo:hi, core, source, at]
            c = remote(block, block, s_outf[k].at[ch, d], r_outf[k].at[ch, d], partner)
            c.start()
            handed[k, ch, d] = c

    def hand(k, ch):
        if not square:
            return
        at = rows(ch, BACK_CHUNKS)
        lo, hi = back_ranges[k]
        for d in reach:
            gather[k, ch, 2 + d].wait_recv()
        block = gathered.at[lo:hi, core, 3 - chip, at]
        c = remote(block, block, s_outf[k].at[ch, 3], r_outf[k].at[ch, 3], partner)
        c.start()
        handed[k, ch, 3] = c

    marked = [0]

    def drain():
        count = marked[0]
        for c in sends[:count]:
            c.wait_send()
        del sends[:count]
        marked[0] = len(sends)

    units = len(out_units)
    for i in range(units + AHEAD + LAG):
        if i < units:
            pair_step(*out_units[i])
        if 0 <= i - AHEAD < units:
            relay_step(*out_units[i - AHEAD])
        if 0 <= i - AHEAD - LAG:
            out_step(*out_units[i - AHEAD - LAG])

    for name, k, ch in ORDER:
        if name == "p":
            if k == 0:
                load_proj.wait()
                for c in load_old:
                    c.wait()
            project(k)
        elif name == "s":
            share(k)
        elif name == "a":
            step(k)
        elif name == "f":
            mix_forward(k)
        elif name == "c":
            combine(k)
        elif name == "u":
            spread(k, ch)
        elif name == "h":
            go_home(k, ch)
        elif name == "k":
            pick(k, ch)
        elif name == "g":
            pass_on(k, ch)
        elif name == "d":
            hand(k, ch)
        elif name == "w":
            drain()

    for c in handed.values():
        c.wait_recv()
    sends += list(gather.values()) + list(handed.values())
    for c in copies:
        c.wait()
    for c in sends:
        c.wait_send()
    for sent, c in guarded:

        @pl.when(sent)
        def _():
            c.wait_send()


def out_bounds(mats, cap, owners):
    ends = [min(mats - cap + 1, owners)]
    for k in range(1, cap):
        ends.append(min(mats - cap + 1 + k, owners * (k + 1)))
    ends[-1] = mats
    return ends


def back_bounds(mats, cap):
    return [-(-mats * (k + 1) // cap) for k in range(cap)]


def steps(text):
    listed = []
    for token in text:
        if len(token) == 3:
            listed.append((token[0], int(token[1]), int(token[2])))
        elif token[0] in "uhkgd":
            listed += [(token[0], int(token[1]), ch) for ch in range(BACK_CHUNKS)]
        else:
            listed.append((token[0], int(token[1]), 0))
    return listed


ORDER = steps((
    "p0", "w0", "s0", "p1", "s1", "a0", "p2", "s2", "a1", "f0", "c0", "u0", "w0", "a2", "f1", "c1", "u1", "h0",
    "f2", "c2", "u2", "h1", "w0", "k0", "g0", "h2", "k1", "d0", "g1", "w0", "k2", "d1", "g2", "d2",
))


def settle(plan, gathered, first, second, out, first_out, second_out, sem):
    mats = out.shape[0]
    _, _, position = places_of(plan, mats)
    copies = []
    for j in range(mats):
        copies.append(pltpu.make_async_copy(gathered.at[position[j]], out.at[j], sem.at[j]))
    copies.append(pltpu.make_async_copy(first, first_out, sem.at[mats]))
    copies.append(pltpu.make_async_copy(second, second_out, sem.at[mats + 1]))
    for c in copies:
        c.start()
    for c in copies:
        c.wait()


def local(grads, proj, moment1, moment2, plan):
    n = lax.axis_size("dp")
    m = lax.axis_size("own")
    chips = n // 2
    mats, own_rows, cols = grads.shape[1:]
    cap, held_rows, rank = proj.shape[1:]
    rank_rows = moment1.shape[2]
    piece = held_rows // chips
    g = grads.reshape(mats, 2, chips, piece, cols)
    w = proj.reshape(cap, chips, piece, rank)
    hbm = pl.BlockSpec(memory_space=pltpu.HBM)
    smem = pl.BlockSpec(memory_space=pltpu.SMEM)
    anywhere = pl.BlockSpec(memory_space=pl.ANY)
    dma = pltpu.SemaphoreType.DMA
    share = (cap, rank_rows, cols)
    oc, bc = OUT_CHUNKS, (BACK_CHUNKS,) * cap

    def per_slot(counts, *shape):
        return [dma((c,) + shape) for c in counts]

    outs = (
        jax.ShapeDtypeStruct(g.shape, BF16),
        jax.ShapeDtypeStruct(share, F32),
        jax.ShapeDtypeStruct(share, F32),
    )
    gathered, first, second = pl.pallas_call(
        functools.partial(kernel, n, m),
        out_shape=outs,
        in_specs=[smem, hbm, hbm, hbm, hbm],
        out_specs=(anywhere, anywhere, anywhere),
        scratch_shapes=[
            pltpu.VMEM((mats, chips, piece, cols), BF16),
            pltpu.VMEM((mats, chips, piece, cols), BF16),
            pltpu.VMEM((mats, chips, piece, cols), BF16),
            pltpu.VMEM((mats, chips, piece, cols), BF16),
            pltpu.VMEM((chips, mats, piece, cols), BF16),
            pltpu.VMEM((chips - 1, mats, piece, cols), BF16),
            pltpu.VMEM((2, mats, piece, cols), BF16),
            pltpu.VMEM((mats, piece, cols), BF16),
            pltpu.VMEM((cap, m, piece, cols), BF16),
            pltpu.VMEM((cap, chips, piece, cols), BF16),
            pltpu.VMEM((cap, chips, piece, rank), BF16),
            pltpu.VMEM((2, cap, chips, rank_rows, cols), BF16),
            pltpu.VMEM((cap, chips, rank_rows, cols), BF16),
            pltpu.VMEM((cap, chips, rank_rows, cols), BF16),
            pltpu.VMEM((cap, chips - 1, rank_rows, cols), BF16),
            pltpu.VMEM((cap, n, 2, rank_rows, cols), BF16),
            pltpu.VMEM((cap, chips, piece, cols), BF16),
            pltpu.VMEM((cap, chips, piece, cols), BF16),
            [[pltpu.VMEM((m, piece // BACK_CHUNKS, cols), BF16)] * BACK_CHUNKS] * cap,
            pltpu.VMEM((mats, piece, cols), BF16),
            pltpu.VMEM((2, cap, rank_rows, cols), F32),
            pltpu.VMEM((2, cap, rank_rows, cols), F32),
            dma((5,)), dma((2, cap)), per_slot(bc),
            per_slot(oc), per_slot(oc),
            per_slot(oc, chips + 2), per_slot(oc, chips + 2),
            per_slot(oc, m), per_slot(oc, chips),
            dma((cap,)), dma((cap,)),
            dma((cap, chips)), dma((cap, chips)),
            dma((cap, chips)), dma((cap, chips)),
            dma((cap, chips)), dma((cap, chips)),
            per_slot(bc, chips), per_slot(bc, chips),
            per_slot(bc, m), per_slot(bc, m),
            per_slot(bc, chips), per_slot(bc, chips),
            per_slot(bc, chips), per_slot(bc, chips),
            per_slot(bc, chips), per_slot(bc, chips),
        ],
        compiler_params=pltpu.CompilerParams(
            collective_id=0, has_side_effects=True, vmem_limit_bytes=44 * 2**20
        ),
    )(*(pltpu.with_memory_space_constraint(x, pltpu.HBM) for x in (plan, g, w, moment1[0], moment2[0])))
    update, first, second = pl.pallas_call(
        settle,
        out_shape=outs,
        in_specs=[smem, anywhere, anywhere, anywhere],
        out_specs=(anywhere, anywhere, anywhere),
        scratch_shapes=[dma((mats + 2,))],
        compiler_params=pltpu.CompilerParams(vmem_limit_bytes=2**20),
    )(pltpu.with_memory_space_constraint(plan, pltpu.HBM), gathered, first, second)
    return (update.reshape(mats, own_rows, cols), first[None], second[None])


def solution(mesh):
    return jax.shard_map(
        local,
        mesh=mesh,
        in_specs=(
            P("dp", None, "own", None),
            P("own", None, "dp", None),
            P("own", None, "dp", None),
            P("own", None, "dp", None),
            P(),
        ),
        out_specs=(P(None, "own", None), P("own", None, "dp", None), P("own", None, "dp", None)),
        check_vma=False,
    )
```

```python
import functools
import jax
import jax.numpy as jnp
from jax import lax
from jax.experimental import pallas as pl
from jax.experimental.pallas import tpu as pltpu
from jax.sharding import PartitionSpec as P

beta_one = 0.9
beta_two = 0.999
adam_eps = 1e-08
norm_eps = 1e-06
correct_one = 1.0 - 0.9**10
correct_two = 1.0 - 0.999**10

OUT_CHUNKS = (4, 2, 2)
DIRECT = ((2, 1),)
AHEAD = 3
LAG = 2
BACK_CHUNKS = 2
F32 = jnp.float32
BF16 = jnp.bfloat16
MESH = pl.DeviceIdType.MESH


def places_of(plan, mats):
    owner = [plan[j] for j in range(mats)]
    within = []
    for j in range(mats):
        before = jnp.int32(0)
        for i in range(j):
            before = before + jnp.where(owner[i] == owner[j], 1, 0)
        within.append(before)
    position = []
    for j in range(mats):
        ahead = jnp.int32(0)
        for i in range(mats):
            if i < j:
                ahead = ahead + jnp.where(within[i] <= within[j], 1, 0)
            elif i > j:
                ahead = ahead + jnp.where(within[i] < within[j], 1, 0)
        position.append(ahead)
    return owner, within, position


def kernel(
    n, m, plan, grads, proj, m1_ref, m2_ref, gathered, m1_out, m2_out,
    held_core, held_other, pair_out, pair_in, half_sum, chip_in, mid_in, total, slot_out, grad, weights,
    part, part_in, pair_sum, share_in, mixed, update, row_in, plane_in, picked,
    old, moments,
    load_sem, moment_sem, local_sem,
    s_pair, r_pair, s_chip, r_chip, s_slot, r_slot,
    s_part, r_part, s_share, r_share, s_mix, r_mix, s_mixf, r_mixf,
    s_back, r_back, s_home, r_home, s_out, r_out, s_diag, r_diag, s_outf, r_outf,
):
    mats = grads.shape[0]
    chips = n // 2
    piece = grads.shape[3]
    cap = m1_ref.shape[0]
    rank_rows = m1_ref.shape[1]
    cols = m1_ref.shape[2]
    rank = n * rank_rows
    dp = lax.axis_index("dp")
    own = lax.axis_index("own")
    core = lax.rem(dp, 2)
    chip = lax.div(dp, 2)
    other = 1 - core
    partner = (2 * chip + other, own)
    out_ends = out_bounds(mats, cap, m)
    back_ends = back_bounds(mats, cap)
    out_ranges = list(zip([0] + out_ends[:-1], out_ends))
    back_ranges = list(zip([0] + back_ends[:-1], back_ends))

    def at_chip(which):
        return (2 * which + core, own)

    square = chips == 4
    reach = (1, 2) if square else tuple(range(1, chips))

    def away(d):
        if not square:
            return lax.rem(chip + d, chips)
        return chip + 1 - 2 * lax.rem(chip, 2) if d == 1 else lax.rem(chip + 2, chips)

    def two_steps(k, ch):
        return square and (k, ch) not in DIRECT

    def from_(d):
        return away(d) if square else lax.rem(chip + chips - d, chips)

    def remote(src, dst, send, recv, device):
        return pltpu.make_async_remote_copy(
            src_ref=src, dst_ref=dst, send_sem=send, recv_sem=recv,
            device_id=device, device_id_type=MESH,
        )

    def rows(ch, count):
        size = piece // count
        return pl.ds(ch * size, size)

    barrier = pltpu.get_barrier_semaphore()

    def plane_at(i):
        h = m // 2
        half = lax.div(own, h)
        if i < m - h:
            return (1 - half) * h + lax.rem(own + i, h)
        return half * h + lax.rem(own + i - h + 1, h)

    greeted = [(dp, lax.rem(own + d, m)) for d in range(1, m)]
    greeted += [at_chip(lax.rem(chip + d, chips)) for d in range(1, chips)] + [partner]
    for device in greeted:
        pl.semaphore_signal(barrier, inc=1, device_id=device, device_id_type=MESH)

    load_other = pltpu.make_async_copy(grads.at[:, other], held_other, load_sem.at[0])
    load_other.start()
    load_core = pltpu.make_async_copy(grads.at[:, core], held_core, load_sem.at[1])
    load_core.start()
    load_proj = pltpu.make_async_copy(proj, weights, load_sem.at[2])
    load_proj.start()
    load_old = [
        pltpu.make_async_copy(m1_ref, old.at[0], load_sem.at[3]),
        pltpu.make_async_copy(m2_ref, old.at[1], load_sem.at[4]),
    ]
    for c in load_old:
        c.start()

    owner, within, position = places_of(plan, mats)
    order = []
    for p in range(mats):
        index = jnp.int32(0)
        for j in range(mats):
            index = jnp.where(position[j] == p, j, index)
        order.append(index)

    def occupant(plane, k):
        at = jnp.int32(0)
        valid = jnp.int32(0)
        for j in range(mats):
            here = jnp.logical_and(owner[j] == plane, within[j] == k)
            at = jnp.where(here, position[j], at)
            valid = jnp.where(here, 1, valid)
        return at, valid.astype(F32)

    sends = []
    guarded = []
    out_units = [(g, ch) for g in range(cap) for ch in range(OUT_CHUNKS[g])]

    load_other.wait()
    pair = {}
    first_unit = True
    for g, ch in out_units:
        at = rows(ch, OUT_CHUNKS[g])
        lo, hi = out_ranges[g]
        for p in range(lo, hi):
            pair_out[p, :, at] = held_other[order[p], :, at]
        if first_unit:
            pl.semaphore_wait(barrier, len(greeted))
            first_unit = False
        c = remote(
            pair_out.at[lo:hi, :, at], pair_in.at[lo:hi, :, at],
            s_pair[g].at[ch], r_pair[g].at[ch], partner,
        )
        c.start()
        pair[g, ch] = c
    sends += list(pair.values())

    load_core.wait()
    over = {}

    def halves(g, ch):
        size = piece // OUT_CHUNKS[g]
        return pl.ds(ch * size, size // 2), pl.ds(ch * size + size // 2, size // 2)

    def send_over(g, ch, i, src, dst, device):
        c = remote(src, dst, s_chip[g].at[ch, i], r_chip[g].at[ch, i], device)
        c.start()
        over[g, ch, i] = c
        sends.append(c)

    def pair_step(g, ch):
        at = rows(ch, OUT_CHUNKS[g])
        lo, hi = out_ranges[g]
        pair[g, ch].wait_recv()
        for p in range(lo, hi):

            @pl.loop(0, chips)
            def _(t):
                half_sum[t, p, at] = (
                    held_core[order[p], t, at].astype(F32) + pair_in[p, t, at].astype(F32)
                ).astype(BF16)

        if square:
            a, b = halves(g, ch)
            x, y, diagonal = away(1), away(2), 3 - chip
            for i, to, half, which in ((0, x, a, diagonal), (1, y, b, diagonal)):
                send_over(
                    g, ch, i, half_sum.at[which, lo:hi, half], mid_in.at[i, lo:hi, half], at_chip(to)
                )
            for i, to, half in ((2, x, a), (3, y, b)):
                send_over(
                    g, ch, i, half_sum.at[to, lo:hi, half], chip_in.at[i - 2, lo:hi, half], at_chip(to)
                )
        else:
            for d in range(1, chips):
                to = away(d)
                send_over(
                    g, ch, d, half_sum.at[to, lo:hi, at], chip_in.at[d - 1, lo:hi, at], at_chip(to)
                )

    def relay_step(g, ch):
        if not square:
            return
        lo, hi = out_ranges[g]
        a, b = halves(g, ch)
        for i, to, half in ((0, away(2), a), (1, away(1), b)):
            over[g, ch, i].wait_recv()
            for p in range(lo, hi):
                half_sum[to, p, half] = (
                    half_sum[to, p, half].astype(F32) + mid_in[i, p, half].astype(F32)
                ).astype(BF16)
            send_over(
                g, ch, 4 + i, half_sum.at[to, lo:hi, half], chip_in.at[1 - i, lo:hi, half], at_chip(to)
            )

    def out_step(g, ch):
        count = OUT_CHUNKS[g]
        at = rows(ch, count)
        lo, hi = out_ranges[g]
        for i in (2, 3, 4, 5) if square else range(1, chips):
            over[g, ch, i].wait_recv()
        for p in range(lo, hi):
            acc = half_sum[chip, p, at].astype(F32)
            for d in reach:
                acc = acc + chip_in[d - 1, p, at].astype(F32)
            total[p, at] = acc.astype(BF16)
        for i in range(m):
            z = plane_at(i)
            index, valid = occupant(z, g)
            slot_out[g, z, at] = (total[index, at].astype(F32) * valid).astype(BF16)
            c = remote(
                slot_out.at[g, z, at], grad.at[g, chip, at],
                s_slot[g].at[ch, i], r_slot[g].at[ch, chip], (2 * own + core, z),
            )
            mine = jnp.logical_and(own == z, chip == own)

            @pl.when(jnp.logical_not(mine))
            def _():
                c.start()

            @pl.when(mine)
            def _():
                grad[g, chip, at] = slot_out[g, z, at]

            guarded.append((jnp.logical_not(mine), c))

    parts = {}
    shares = {}
    combined = {}
    scale = {}
    mix = {}
    forward = {}
    back = {}
    home = {}
    gather = {}
    handed = {}
    copies = []

    def project(k):
        count = OUT_CHUNKS[k]
        for ch in range(count):
            for source in range(chips):
                at = rows(ch, count)
                c = remote(
                    slot_out.at[k, 0, at], grad.at[k, source, at],
                    s_slot[k].at[ch, 0], r_slot[k].at[ch, source], (dp, own),
                )

                @pl.when(jnp.logical_not(jnp.logical_and(chip == own, source == chip)))
                def _():
                    c.wait_recv()

        g = grad[k].reshape(chips * piece, cols)
        w = weights[k].reshape(chips * piece, rank)
        value = lax.dot_general(g, w, (((0,), (0,)), ((), ())), preferred_element_type=F32)
        value = value.T.astype(BF16)
        for t in range(chips):
            for s in range(2):
                at = (2 * t + s) * rank_rows
                part[s, k, t] = value[at : at + rank_rows]
        c = remote(part.at[other, k], part_in.at[k], s_part.at[k], r_part.at[k], partner)
        c.start()
        parts[k] = c
        sends.append(c)

    def share(k):
        parts[k].wait_recv()
        for t in range(chips):
            pair_sum[k, t] = (part[core, k, t].astype(F32) + part_in[k, t].astype(F32)).astype(BF16)
        for d in range(1, chips):
            to = lax.rem(chip + d, chips)
            c = remote(
                pair_sum.at[k, to], share_in.at[k, d - 1],
                s_share.at[k, d], r_share.at[k, d], at_chip(to),
            )
            c.start()
            shares[k, d] = c
            sends.append(c)

    def step(k):
        for d in range(1, chips):
            shares[k, d].wait_recv()
        value = pair_sum[k, chip].astype(F32)
        for d in range(1, chips):
            value = value + share_in[k, d - 1].astype(F32)
        first = beta_one * old[0, k] + (1.0 - beta_one) * value
        second = beta_two * old[1, k] + (1.0 - beta_two) * value * value
        moments[0, k] = first
        moments[1, k] = second
        taken = first / correct_one / (jnp.sqrt(second / correct_two) + adam_eps)
        mixed[k, dp, 0] = taken.astype(BF16)
        mixed[k, dp, 1] = value.astype(BF16)
        for d in range(1, chips):
            to = lax.rem(chip + d, chips)
            c = remote(mixed.at[k, dp], mixed.at[k, dp], s_mix.at[k, d], r_mix.at[k, d], at_chip(to))
            c.start()
            mix[k, d] = c
            sends.append(c)
        c = remote(mixed.at[k, dp], mixed.at[k, dp], s_mixf.at[k, 0], r_mixf.at[k, 0], partner)
        c.start()
        forward[k, 0] = c
        sends.append(c)
        for i, target in ((0, m1_out), (1, m2_out)):
            c = pltpu.make_async_copy(moments.at[i, k], target.at[k], moment_sem.at[i, k])
            c.start()
            copies.append(c)

    def mix_forward(k):
        for d in range(1, chips):
            mix[k, d].wait_recv()
            at = 2 * lax.rem(chip + chips - d, chips) + core
            c = remote(mixed.at[k, at], mixed.at[k, at], s_mixf.at[k, d], r_mixf.at[k, d], partner)
            c.start()
            forward[k, d] = c
            sends.append(c)

    def combine(k):
        for d in range(chips):
            forward[k, d].wait_recv()
        taken = mixed[k, :, 0].reshape(rank, cols).astype(F32)
        value = mixed[k, :, 1].reshape(rank, cols).astype(F32)
        grad_sum = jnp.sum(value * value, axis=0, keepdims=True)
        step_sum = jnp.sum(taken * taken, axis=0, keepdims=True)
        scale[k] = jnp.sqrt(step_sum) / (jnp.sqrt(grad_sum) + norm_eps)
        combined[k] = (taken - scale[k] * value).astype(BF16)

    def spread(k, ch):
        count = BACK_CHUNKS
        size = piece // count
        at = rows(ch, count)
        w = weights[k, :, at].reshape(chips * size, rank)
        value = jnp.dot(w, combined[k], preferred_element_type=F32)
        g = grad[k, :, at].reshape(chips * size, cols).astype(F32)
        value = (value + scale[k] * g).astype(BF16)
        for t in range(chips):
            update[k, t, at] = value[t * size : (t + 1) * size]
        for d in range(1, chips):
            to = lax.rem(chip + d, chips)
            c = remote(
                update.at[k, to, at], row_in.at[k, chip, at],
                s_back[k].at[ch, d], r_back[k].at[ch, d], at_chip(to),
            )
            c.start()
            back[k, ch, d] = c
            sends.append(c)
        row_in[k, chip, at] = update[k, chip, at]

    def go_home(k, ch):
        at = rows(ch, BACK_CHUNKS)
        for d in range(1, chips):
            back[k, ch, d].wait_recv()
        for dz in range(m - 1):
            to = plane_at(dz)
            c = remote(
                row_in.at[k, to, at], plane_in[k][ch].at[own],
                s_home[k].at[ch, dz], r_home[k].at[ch, dz], (dp, to),
            )
            c.start()
            home[k, ch, dz] = c
            sends.append(c)
        plane_in[k][ch][own] = row_in[k, own, at]

    def pick(k, ch):
        count = BACK_CHUNKS
        at = rows(ch, count)
        for dz in range(m - 1):
            home[k, ch, dz].wait_recv()
        lo, hi = back_ranges[k]
        for p in range(lo, hi):
            who = jnp.int32(0)
            slot = jnp.int32(0)
            for j in range(mats):
                who = jnp.where(position[j] == p, owner[j], who)
                slot = jnp.where(position[j] == p, within[j], slot)
            value = plane_in[0][ch][who]
            for i in range(1, k + 1):
                value = jnp.where(slot == i, plane_in[i][ch][who], value)
            picked[p, at] = value
        for d in reach if two_steps(k, ch) else range(1, chips):
            to = away(d) if two_steps(k, ch) else lax.rem(chip + d, chips)
            c = remote(
                picked.at[lo:hi, at], gathered.at[lo:hi, core, chip, at],
                s_out[k].at[ch, d], r_out[k].at[ch, d], at_chip(to),
            )
            c.start()
            gather[k, ch, d] = c
        c = remote(
            picked.at[lo:hi, at], gathered.at[lo:hi, core, chip, at],
            s_outf[k].at[ch, 0], r_outf[k].at[ch, 0], partner,
        )
        c.start()
        handed[k, ch, 0] = c
        c = pltpu.make_async_copy(
            picked.at[lo:hi, at], gathered.at[lo:hi, core, chip, at], local_sem[k].at[ch]
        )
        c.start()
        copies.append(c)

    def pass_on(k, ch):
        at = rows(ch, BACK_CHUNKS)
        half = piece // BACK_CHUNKS // 2
        lo, hi = back_ranges[k]
        for d in reach if two_steps(k, ch) else range(1, chips):
            gather[k, ch, d].wait_recv()
            source = from_(d) if two_steps(k, ch) else lax.rem(chip + chips - d, chips)
            if two_steps(k, ch):
                part_at = pl.ds(ch * 2 * half + (half if d == 2 else 0), half)
                block = gathered.at[lo:hi, core, source, part_at]
                c = remote(
                    block, block, s_diag[k].at[ch, d], r_diag[k].at[ch, d], at_chip(away(3 - d))
                )
                c.start()
                gather[k, ch, 2 + d] = c
            block = gathered.at[lo:hi, core, source, at]
            c = remote(block, block, s_outf[k].at[ch, d], r_outf[k].at[ch, d], partner)
            c.start()
            handed[k, ch, d] = c

    def hand(k, ch):
        if not two_steps(k, ch):
            return
        at = rows(ch, BACK_CHUNKS)
        lo, hi = back_ranges[k]
        for d in reach:
            gather[k, ch, 2 + d].wait_recv()
        block = gathered.at[lo:hi, core, 3 - chip, at]
        c = remote(block, block, s_outf[k].at[ch, 3], r_outf[k].at[ch, 3], partner)
        c.start()
        handed[k, ch, 3] = c

    marked = [0]

    def drain():
        count = marked[0]
        for c in sends[:count]:
            c.wait_send()
        del sends[:count]
        marked[0] = len(sends)

    units = len(out_units)
    for i in range(units + AHEAD + LAG):
        if i < units:
            pair_step(*out_units[i])
        if 0 <= i - AHEAD < units:
            relay_step(*out_units[i - AHEAD])
        if 0 <= i - AHEAD - LAG:
            out_step(*out_units[i - AHEAD - LAG])

    for name, k, ch in ORDER:
        if name == "p":
            if k == 0:
                load_proj.wait()
                for c in load_old:
                    c.wait()
            project(k)
        elif name == "s":
            share(k)
        elif name == "a":
            step(k)
        elif name == "f":
            mix_forward(k)
        elif name == "c":
            combine(k)
        elif name == "u":
            spread(k, ch)
        elif name == "h":
            go_home(k, ch)
        elif name == "k":
            pick(k, ch)
        elif name == "g":
            pass_on(k, ch)
        elif name == "d":
            hand(k, ch)
        elif name == "w":
            drain()

    for c in handed.values():
        c.wait_recv()
    sends += list(gather.values()) + list(handed.values())
    for c in copies:
        c.wait()
    for c in sends:
        c.wait_send()
    for sent, c in guarded:

        @pl.when(sent)
        def _():
            c.wait_send()


def out_bounds(mats, cap, owners):
    ends = [min(mats - cap + 1, owners)]
    for k in range(1, cap):
        ends.append(min(mats - cap + 1 + k, owners * (k + 1)))
    ends[-1] = mats
    return ends


def back_bounds(mats, cap):
    return [-(-mats * (k + 1) // cap) for k in range(cap)]


def steps(text):
    listed = []
    for token in text:
        if len(token) == 3:
            listed.append((token[0], int(token[1]), int(token[2])))
        elif token[0] in "uhkgd":
            listed += [(token[0], int(token[1]), ch) for ch in range(BACK_CHUNKS)]
        else:
            listed.append((token[0], int(token[1]), 0))
    return listed


ORDER = steps((
    "p0", "w0", "s0", "p1", "s1", "a0", "p2", "s2", "a1", "f0", "c0", "u0", "w0", "a2", "f1", "c1", "u1", "h0",
    "f2", "c2", "u2", "h1", "w0", "k0", "g0", "h2", "k1", "d0", "g1", "w0", "k2", "d1", "g2", "d2",
))


def settle(plan, gathered, first, second, out, first_out, second_out, sem):
    mats = out.shape[0]
    _, _, position = places_of(plan, mats)
    copies = []
    for j in range(mats):
        copies.append(pltpu.make_async_copy(gathered.at[position[j]], out.at[j], sem.at[j]))
    copies.append(pltpu.make_async_copy(first, first_out, sem.at[mats]))
    copies.append(pltpu.make_async_copy(second, second_out, sem.at[mats + 1]))
    for c in copies:
        c.start()
    for c in copies:
        c.wait()


def local(grads, proj, moment1, moment2, plan):
    n = lax.axis_size("dp")
    m = lax.axis_size("own")
    chips = n // 2
    mats, own_rows, cols = grads.shape[1:]
    cap, held_rows, rank = proj.shape[1:]
    rank_rows = moment1.shape[2]
    piece = held_rows // chips
    g = grads.reshape(mats, 2, chips, piece, cols)
    w = proj.reshape(cap, chips, piece, rank)
    hbm = pl.BlockSpec(memory_space=pltpu.HBM)
    smem = pl.BlockSpec(memory_space=pltpu.SMEM)
    anywhere = pl.BlockSpec(memory_space=pl.ANY)
    dma = pltpu.SemaphoreType.DMA
    share = (cap, rank_rows, cols)
    oc, bc = OUT_CHUNKS, (BACK_CHUNKS,) * cap

    def per_slot(counts, *shape):
        return [dma((c,) + shape) for c in counts]

    outs = (
        jax.ShapeDtypeStruct(g.shape, BF16),
        jax.ShapeDtypeStruct(share, F32),
        jax.ShapeDtypeStruct(share, F32),
    )
    gathered, first, second = pl.pallas_call(
        functools.partial(kernel, n, m),
        out_shape=outs,
        in_specs=[smem, hbm, hbm, hbm, hbm],
        out_specs=(anywhere, anywhere, anywhere),
        scratch_shapes=[
            pltpu.VMEM((mats, chips, piece, cols), BF16),
            pltpu.VMEM((mats, chips, piece, cols), BF16),
            pltpu.VMEM((mats, chips, piece, cols), BF16),
            pltpu.VMEM((mats, chips, piece, cols), BF16),
            pltpu.VMEM((chips, mats, piece, cols), BF16),
            pltpu.VMEM((chips - 1, mats, piece, cols), BF16),
            pltpu.VMEM((2, mats, piece, cols), BF16),
            pltpu.VMEM((mats, piece, cols), BF16),
            pltpu.VMEM((cap, m, piece, cols), BF16),
            pltpu.VMEM((cap, chips, piece, cols), BF16),
            pltpu.VMEM((cap, chips, piece, rank), BF16),
            pltpu.VMEM((2, cap, chips, rank_rows, cols), BF16),
            pltpu.VMEM((cap, chips, rank_rows, cols), BF16),
            pltpu.VMEM((cap, chips, rank_rows, cols), BF16),
            pltpu.VMEM((cap, chips - 1, rank_rows, cols), BF16),
            pltpu.VMEM((cap, n, 2, rank_rows, cols), BF16),
            pltpu.VMEM((cap, chips, piece, cols), BF16),
            pltpu.VMEM((cap, chips, piece, cols), BF16),
            [[pltpu.VMEM((m, piece // BACK_CHUNKS, cols), BF16)] * BACK_CHUNKS] * cap,
            pltpu.VMEM((mats, piece, cols), BF16),
            pltpu.VMEM((2, cap, rank_rows, cols), F32),
            pltpu.VMEM((2, cap, rank_rows, cols), F32),
            dma((5,)), dma((2, cap)), per_slot(bc),
            per_slot(oc), per_slot(oc),
            per_slot(oc, chips + 2), per_slot(oc, chips + 2),
            per_slot(oc, m), per_slot(oc, chips),
            dma((cap,)), dma((cap,)),
            dma((cap, chips)), dma((cap, chips)),
            dma((cap, chips)), dma((cap, chips)),
            dma((cap, chips)), dma((cap, chips)),
            per_slot(bc, chips), per_slot(bc, chips),
            per_slot(bc, m), per_slot(bc, m),
            per_slot(bc, chips), per_slot(bc, chips),
            per_slot(bc, chips), per_slot(bc, chips),
            per_slot(bc, chips), per_slot(bc, chips),
        ],
        compiler_params=pltpu.CompilerParams(
            collective_id=0, has_side_effects=True, vmem_limit_bytes=44 * 2**20
        ),
    )(*(pltpu.with_memory_space_constraint(x, pltpu.HBM) for x in (plan, g, w, moment1[0], moment2[0])))
    update, first, second = pl.pallas_call(
        settle,
        out_shape=outs,
        in_specs=[smem, anywhere, anywhere, anywhere],
        out_specs=(anywhere, anywhere, anywhere),
        scratch_shapes=[dma((mats + 2,))],
        compiler_params=pltpu.CompilerParams(vmem_limit_bytes=2**20),
    )(pltpu.with_memory_space_constraint(plan, pltpu.HBM), gathered, first, second)
    return (update.reshape(mats, own_rows, cols), first[None], second[None])


def solution(mesh):
    return jax.shard_map(
        local,
        mesh=mesh,
        in_specs=(
            P("dp", None, "own", None),
            P("own", None, "dp", None),
            P("own", None, "dp", None),
            P("own", None, "dp", None),
            P(),
        ),
        out_specs=(P(None, "own", None), P("own", None, "dp", None), P("own", None, "dp", None)),
        check_vma=False,
    )
```

```python
import functools
import jax
import jax.numpy as jnp
from jax import lax
from jax.experimental import pallas as pl
from jax.experimental.pallas import tpu as pltpu
from jax.sharding import PartitionSpec as P

beta_one = 0.9
beta_two = 0.999
adam_eps = 1e-08
norm_eps = 1e-06
correct_one = 1.0 - 0.9**10
correct_two = 1.0 - 0.999**10

OUT_CHUNKS = (4, 2, 2)
DIRECT = ((2, 1),)
AHEAD = 3
LAG = 2
BACK_CHUNKS = 2
F32 = jnp.float32
BF16 = jnp.bfloat16
MESH = pl.DeviceIdType.MESH


def places_of(plan, mats):
    owner = [plan[j] for j in range(mats)]
    within = []
    for j in range(mats):
        before = jnp.int32(0)
        for i in range(j):
            before = before + jnp.where(owner[i] == owner[j], 1, 0)
        within.append(before)
    position = []
    for j in range(mats):
        ahead = jnp.int32(0)
        for i in range(mats):
            if i < j:
                ahead = ahead + jnp.where(within[i] <= within[j], 1, 0)
            elif i > j:
                ahead = ahead + jnp.where(within[i] < within[j], 1, 0)
        position.append(ahead)
    return owner, within, position


def kernel(
    n, m, plan, grads, proj, m1_ref, m2_ref, gathered, m1_out, m2_out,
    held_core, held_other, pair_out, pair_in, half_sum, chip_in, mid_in, total, slot_out, grad, weights,
    part, part_in, pair_sum, share_in, mixed, update, row_in, plane_in, picked,
    old, moments,
    load_sem, moment_sem, local_sem,
    s_pair, r_pair, s_chip, r_chip, s_slot, r_slot,
    s_part, r_part, s_share, r_share, s_mix, r_mix, s_mixf, r_mixf,
    s_back, r_back, s_home, r_home, s_out, r_out, s_diag, r_diag, s_outf, r_outf,
):
    mats = grads.shape[0]
    chips = n // 2
    piece = grads.shape[3]
    cap = m1_ref.shape[0]
    rank_rows = m1_ref.shape[1]
    cols = m1_ref.shape[2]
    rank = n * rank_rows
    dp = lax.axis_index("dp")
    own = lax.axis_index("own")
    core = lax.rem(dp, 2)
    chip = lax.div(dp, 2)
    other = 1 - core
    partner = (2 * chip + other, own)
    out_ends = out_bounds(mats, cap, m)
    back_ends = back_bounds(mats, cap)
    out_ranges = list(zip([0] + out_ends[:-1], out_ends))
    back_ranges = list(zip([0] + back_ends[:-1], back_ends))

    def at_chip(which):
        return (2 * which + core, own)

    square = chips == 4
    reach = (1, 2) if square else tuple(range(1, chips))

    def away(d):
        if not square:
            return lax.rem(chip + d, chips)
        return chip + 1 - 2 * lax.rem(chip, 2) if d == 1 else lax.rem(chip + 2, chips)

    def two_steps(k, ch):
        return square and (k, ch) not in DIRECT

    def from_(d):
        return away(d) if square else lax.rem(chip + chips - d, chips)

    def remote(src, dst, send, recv, device):
        return pltpu.make_async_remote_copy(
            src_ref=src, dst_ref=dst, send_sem=send, recv_sem=recv,
            device_id=device, device_id_type=MESH,
        )

    def rows(ch, count):
        size = piece // count
        return pl.ds(ch * size, size)

    barrier = pltpu.get_barrier_semaphore()

    def plane_at(i):
        h = m // 2
        half = lax.div(own, h)
        if i < m - h:
            return (1 - half) * h + lax.rem(own + i, h)
        return half * h + lax.rem(own + i - h + 1, h)

    greeted = [(dp, lax.rem(own + d, m)) for d in range(1, m)]
    greeted += [at_chip(lax.rem(chip + d, chips)) for d in range(1, chips)] + [partner]
    for device in greeted:
        pl.semaphore_signal(barrier, inc=1, device_id=device, device_id_type=MESH)

    load_other = pltpu.make_async_copy(grads.at[:, other], held_other, load_sem.at[0])
    load_other.start()
    load_core = pltpu.make_async_copy(grads.at[:, core], held_core, load_sem.at[1])
    load_core.start()
    load_proj = pltpu.make_async_copy(proj, weights, load_sem.at[2])
    load_proj.start()
    load_old = [
        pltpu.make_async_copy(m1_ref, old.at[0], load_sem.at[3]),
        pltpu.make_async_copy(m2_ref, old.at[1], load_sem.at[4]),
    ]
    for c in load_old:
        c.start()

    owner, within, position = places_of(plan, mats)
    order = []
    for p in range(mats):
        index = jnp.int32(0)
        for j in range(mats):
            index = jnp.where(position[j] == p, j, index)
        order.append(index)

    def occupant(plane, k):
        at = jnp.int32(0)
        valid = jnp.int32(0)
        for j in range(mats):
            here = jnp.logical_and(owner[j] == plane, within[j] == k)
            at = jnp.where(here, position[j], at)
            valid = jnp.where(here, 1, valid)
        return at, valid.astype(F32)

    sends = []
    guarded = []
    out_units = [(g, ch) for g in range(cap) for ch in range(OUT_CHUNKS[g])]

    load_other.wait()
    pair = {}
    first_unit = True
    for g, ch in out_units:
        at = rows(ch, OUT_CHUNKS[g])
        lo, hi = out_ranges[g]
        for p in range(lo, hi):
            pair_out[p, :, at] = held_other[order[p], :, at]
        if first_unit:
            pl.semaphore_wait(barrier, len(greeted))
            first_unit = False
        c = remote(
            pair_out.at[lo:hi, :, at], pair_in.at[lo:hi, :, at],
            s_pair[g].at[ch], r_pair[g].at[ch], partner,
        )
        c.start()
        pair[g, ch] = c
    sends += list(pair.values())

    load_core.wait()
    over = {}

    def halves(g, ch):
        size = piece // OUT_CHUNKS[g]
        return pl.ds(ch * size, size // 2), pl.ds(ch * size + size // 2, size // 2)

    def send_over(g, ch, i, src, dst, device):
        c = remote(src, dst, s_chip[g].at[ch, i], r_chip[g].at[ch, i], device)
        c.start()
        over[g, ch, i] = c
        sends.append(c)

    def pair_step(g, ch):
        at = rows(ch, OUT_CHUNKS[g])
        lo, hi = out_ranges[g]
        pair[g, ch].wait_recv()
        for p in range(lo, hi):

            @pl.loop(0, chips)
            def _(t):
                half_sum[t, p, at] = (
                    held_core[order[p], t, at].astype(F32) + pair_in[p, t, at].astype(F32)
                ).astype(BF16)

        if square:
            a, b = halves(g, ch)
            x, y, diagonal = away(1), away(2), 3 - chip
            for i, to, half, which in ((0, x, a, diagonal), (1, y, b, diagonal)):
                send_over(
                    g, ch, i, half_sum.at[which, lo:hi, half], mid_in.at[i, lo:hi, half], at_chip(to)
                )
            for i, to, half in ((2, x, a), (3, y, b)):
                send_over(
                    g, ch, i, half_sum.at[to, lo:hi, half], chip_in.at[i - 2, lo:hi, half], at_chip(to)
                )
        else:
            for d in range(1, chips):
                to = away(d)
                send_over(
                    g, ch, d, half_sum.at[to, lo:hi, at], chip_in.at[d - 1, lo:hi, at], at_chip(to)
                )

    def relay_step(g, ch):
        if not square:
            return
        lo, hi = out_ranges[g]
        a, b = halves(g, ch)
        for i, to, half in ((0, away(2), a), (1, away(1), b)):
            over[g, ch, i].wait_recv()
            for p in range(lo, hi):
                half_sum[to, p, half] = (
                    half_sum[to, p, half].astype(F32) + mid_in[i, p, half].astype(F32)
                ).astype(BF16)
            send_over(
                g, ch, 4 + i, half_sum.at[to, lo:hi, half], chip_in.at[1 - i, lo:hi, half], at_chip(to)
            )

    def out_step(g, ch):
        count = OUT_CHUNKS[g]
        at = rows(ch, count)
        lo, hi = out_ranges[g]
        for i in (2, 3, 4, 5) if square else range(1, chips):
            over[g, ch, i].wait_recv()
        for p in range(lo, hi):
            acc = half_sum[chip, p, at].astype(F32)
            for d in reach:
                acc = acc + chip_in[d - 1, p, at].astype(F32)
            total[p, at] = acc.astype(BF16)
        for i in range(m):
            z = plane_at(i)
            index, valid = occupant(z, g)
            slot_out[g, z, at] = (total[index, at].astype(F32) * valid).astype(BF16)
            c = remote(
                slot_out.at[g, z, at], grad.at[g, chip, at],
                s_slot[g].at[ch, i], r_slot[g].at[ch, chip], (2 * own + core, z),
            )
            mine = jnp.logical_and(own == z, chip == own)

            @pl.when(jnp.logical_not(mine))
            def _():
                c.start()

            @pl.when(mine)
            def _():
                grad[g, chip, at] = slot_out[g, z, at]

            guarded.append((jnp.logical_not(mine), c))

    parts = {}
    shares = {}
    combined = {}
    scale = {}
    mix = {}
    forward = {}
    back = {}
    home = {}
    gather = {}
    handed = {}
    copies = []

    def project(k):
        count = OUT_CHUNKS[k]
        for ch in range(count):
            for source in range(chips):
                at = rows(ch, count)
                c = remote(
                    slot_out.at[k, 0, at], grad.at[k, source, at],
                    s_slot[k].at[ch, 0], r_slot[k].at[ch, source], (dp, own),
                )

                @pl.when(jnp.logical_not(jnp.logical_and(chip == own, source == chip)))
                def _():
                    c.wait_recv()

        g = grad[k].reshape(chips * piece, cols)
        w = weights[k].reshape(chips * piece, rank)
        value = lax.dot_general(g, w, (((0,), (0,)), ((), ())), preferred_element_type=F32)
        value = value.T.astype(BF16)
        for t in range(chips):
            for s in range(2):
                at = (2 * t + s) * rank_rows
                part[s, k, t] = value[at : at + rank_rows]
        c = remote(part.at[other, k], part_in.at[k], s_part.at[k], r_part.at[k], partner)
        c.start()
        parts[k] = c
        sends.append(c)

    def share(k):
        parts[k].wait_recv()
        for t in range(chips):
            pair_sum[k, t] = (part[core, k, t].astype(F32) + part_in[k, t].astype(F32)).astype(BF16)
        for d in range(1, chips):
            to = lax.rem(chip + d, chips)
            c = remote(
                pair_sum.at[k, to], share_in.at[k, d - 1],
                s_share.at[k, d], r_share.at[k, d], at_chip(to),
            )
            c.start()
            shares[k, d] = c
            sends.append(c)

    def step(k):
        for d in range(1, chips):
            shares[k, d].wait_recv()
        value = pair_sum[k, chip].astype(F32)
        for d in range(1, chips):
            value = value + share_in[k, d - 1].astype(F32)
        first = beta_one * old[0, k] + (1.0 - beta_one) * value
        second = beta_two * old[1, k] + (1.0 - beta_two) * value * value
        moments[0, k] = first
        moments[1, k] = second
        taken = first / correct_one / (jnp.sqrt(second / correct_two) + adam_eps)
        mixed[k, dp, 0] = taken.astype(BF16)
        mixed[k, dp, 1] = value.astype(BF16)
        for d in range(1, chips):
            to = lax.rem(chip + d, chips)
            c = remote(mixed.at[k, dp], mixed.at[k, dp], s_mix.at[k, d], r_mix.at[k, d], at_chip(to))
            c.start()
            mix[k, d] = c
            sends.append(c)
        c = remote(mixed.at[k, dp], mixed.at[k, dp], s_mixf.at[k, 0], r_mixf.at[k, 0], partner)
        c.start()
        forward[k, 0] = c
        sends.append(c)
        for i, target in ((0, m1_out), (1, m2_out)):
            c = pltpu.make_async_copy(moments.at[i, k], target.at[k], moment_sem.at[i, k])
            c.start()
            copies.append(c)

    def mix_forward(k):
        for d in range(1, chips):
            mix[k, d].wait_recv()
            at = 2 * lax.rem(chip + chips - d, chips) + core
            c = remote(mixed.at[k, at], mixed.at[k, at], s_mixf.at[k, d], r_mixf.at[k, d], partner)
            c.start()
            forward[k, d] = c
            sends.append(c)

    def combine(k):
        for d in range(chips):
            forward[k, d].wait_recv()
        taken = mixed[k, :, 0].reshape(rank, cols).astype(F32)
        value = mixed[k, :, 1].reshape(rank, cols).astype(F32)
        grad_sum = jnp.sum(value * value, axis=0, keepdims=True)
        step_sum = jnp.sum(taken * taken, axis=0, keepdims=True)
        scale[k] = jnp.sqrt(step_sum) / (jnp.sqrt(grad_sum) + norm_eps)
        combined[k] = (taken - scale[k] * value).astype(BF16)

    def spread(k, ch):
        count = BACK_CHUNKS
        size = piece // count
        at = rows(ch, count)
        w = weights[k, :, at].reshape(chips * size, rank)
        value = jnp.dot(w, combined[k], preferred_element_type=F32)
        g = grad[k, :, at].reshape(chips * size, cols).astype(F32)
        value = (value + scale[k] * g).astype(BF16)
        for t in range(chips):
            update[k, t, at] = value[t * size : (t + 1) * size]
        for d in range(1, chips):
            to = lax.rem(chip + d, chips)
            c = remote(
                update.at[k, to, at], row_in.at[k, chip, at],
                s_back[k].at[ch, d], r_back[k].at[ch, d], at_chip(to),
            )
            c.start()
            back[k, ch, d] = c
            sends.append(c)
        row_in[k, chip, at] = update[k, chip, at]

    def go_home(k, ch):
        at = rows(ch, BACK_CHUNKS)
        for d in range(1, chips):
            back[k, ch, d].wait_recv()
        for dz in range(m - 1):
            to = plane_at(dz)
            c = remote(
                row_in.at[k, to, at], plane_in[k][ch].at[own],
                s_home[k].at[ch, dz], r_home[k].at[ch, dz], (dp, to),
            )
            c.start()
            home[k, ch, dz] = c
            sends.append(c)
        plane_in[k][ch][own] = row_in[k, own, at]

    def pick(k, ch):
        count = BACK_CHUNKS
        at = rows(ch, count)
        for dz in range(m - 1):
            home[k, ch, dz].wait_recv()
        lo, hi = back_ranges[k]
        for p in range(lo, hi):
            who = jnp.int32(0)
            slot = jnp.int32(0)
            for j in range(mats):
                who = jnp.where(position[j] == p, owner[j], who)
                slot = jnp.where(position[j] == p, within[j], slot)
            value = plane_in[0][ch][who]
            for i in range(1, k + 1):
                value = jnp.where(slot == i, plane_in[i][ch][who], value)
            picked[p, at] = value
        for d in reach if two_steps(k, ch) else range(1, chips):
            to = away(d) if two_steps(k, ch) else lax.rem(chip + d, chips)
            c = remote(
                picked.at[lo:hi, at], gathered.at[lo:hi, core, chip, at],
                s_out[k].at[ch, d], r_out[k].at[ch, d], at_chip(to),
            )
            c.start()
            gather[k, ch, d] = c
        c = remote(
            picked.at[lo:hi, at], gathered.at[lo:hi, core, chip, at],
            s_outf[k].at[ch, 0], r_outf[k].at[ch, 0], partner,
        )
        c.start()
        handed[k, ch, 0] = c
        c = pltpu.make_async_copy(
            picked.at[lo:hi, at], gathered.at[lo:hi, core, chip, at], local_sem[k].at[ch]
        )
        c.start()
        copies.append(c)

    def pass_on(k, ch):
        at = rows(ch, BACK_CHUNKS)
        half = piece // BACK_CHUNKS // 2
        lo, hi = back_ranges[k]
        for d in reach if two_steps(k, ch) else range(1, chips):
            gather[k, ch, d].wait_recv()
            source = from_(d) if two_steps(k, ch) else lax.rem(chip + chips - d, chips)
            if two_steps(k, ch):
                part_at = pl.ds(ch * 2 * half + (half if d == 2 else 0), half)
                block = gathered.at[lo:hi, core, source, part_at]
                c = remote(
                    block, block, s_diag[k].at[ch, d], r_diag[k].at[ch, d], at_chip(away(3 - d))
                )
                c.start()
                gather[k, ch, 2 + d] = c
            block = gathered.at[lo:hi, core, source, at]
            c = remote(block, block, s_outf[k].at[ch, d], r_outf[k].at[ch, d], partner)
            c.start()
            handed[k, ch, d] = c

    def hand(k, ch):
        if not two_steps(k, ch):
            return
        at = rows(ch, BACK_CHUNKS)
        lo, hi = back_ranges[k]
        for d in reach:
            gather[k, ch, 2 + d].wait_recv()
        block = gathered.at[lo:hi, core, 3 - chip, at]
        c = remote(block, block, s_outf[k].at[ch, 3], r_outf[k].at[ch, 3], partner)
        c.start()
        handed[k, ch, 3] = c

    marked = [0]

    def drain():
        count = marked[0]
        for c in sends[:count]:
            c.wait_send()
        del sends[:count]
        marked[0] = len(sends)

    units = len(out_units)
    for i in range(units + AHEAD + LAG):
        if i < units:
            pair_step(*out_units[i])
        if 0 <= i - AHEAD < units:
            relay_step(*out_units[i - AHEAD])
        if 0 <= i - AHEAD - LAG:
            out_step(*out_units[i - AHEAD - LAG])

    for name, k, ch in ORDER:
        if name == "p":
            if k == 0:
                load_proj.wait()
                for c in load_old:
                    c.wait()
            project(k)
        elif name == "s":
            share(k)
        elif name == "a":
            step(k)
        elif name == "f":
            mix_forward(k)
        elif name == "c":
            combine(k)
        elif name == "u":
            spread(k, ch)
        elif name == "h":
            go_home(k, ch)
        elif name == "k":
            pick(k, ch)
        elif name == "g":
            pass_on(k, ch)
        elif name == "d":
            hand(k, ch)
        elif name == "w":
            drain()

    for c in handed.values():
        c.wait_recv()
    sends += list(gather.values()) + list(handed.values())
    for c in copies:
        c.wait()
    for c in sends:
        c.wait_send()
    for sent, c in guarded:

        @pl.when(sent)
        def _():
            c.wait_send()


def out_bounds(mats, cap, owners):
    ends = [min(mats - cap + 1, owners)]
    for k in range(1, cap):
        ends.append(min(mats - cap + 1 + k, owners * (k + 1)))
    ends[-1] = mats
    return ends


def back_bounds(mats, cap):
    return [-(-mats * (k + 1) // cap) for k in range(cap)]


def steps(text):
    listed = []
    for token in text:
        if len(token) == 3:
            listed.append((token[0], int(token[1]), int(token[2])))
        elif token[0] in "uhkgd":
            listed += [(token[0], int(token[1]), ch) for ch in range(BACK_CHUNKS)]
        else:
            listed.append((token[0], int(token[1]), 0))
    return listed


ORDER = steps((
    "p0", "w0", "s0", "p1", "s1", "a0", "p2", "s2", "a1", "f0", "c0", "u0", "w0", "a2", "f1", "c1", "u1", "h0",
    "f2", "c2", "u2", "h1", "w0", "k0", "g0", "h2", "k1", "d0", "g1", "w0", "k20", "k21", "d1", "g20", "d20", "g21", "d21",
))


def settle(plan, gathered, first, second, out, first_out, second_out, sem):
    mats = out.shape[0]
    _, _, position = places_of(plan, mats)
    copies = []
    for j in range(mats):
        copies.append(pltpu.make_async_copy(gathered.at[position[j]], out.at[j], sem.at[j]))
    copies.append(pltpu.make_async_copy(first, first_out, sem.at[mats]))
    copies.append(pltpu.make_async_copy(second, second_out, sem.at[mats + 1]))
    for c in copies:
        c.start()
    for c in copies:
        c.wait()


def local(grads, proj, moment1, moment2, plan):
    n = lax.axis_size("dp")
    m = lax.axis_size("own")
    chips = n // 2
    mats, own_rows, cols = grads.shape[1:]
    cap, held_rows, rank = proj.shape[1:]
    rank_rows = moment1.shape[2]
    piece = held_rows // chips
    g = grads.reshape(mats, 2, chips, piece, cols)
    w = proj.reshape(cap, chips, piece, rank)
    hbm = pl.BlockSpec(memory_space=pltpu.HBM)
    smem = pl.BlockSpec(memory_space=pltpu.SMEM)
    anywhere = pl.BlockSpec(memory_space=pl.ANY)
    dma = pltpu.SemaphoreType.DMA
    share = (cap, rank_rows, cols)
    oc, bc = OUT_CHUNKS, (BACK_CHUNKS,) * cap

    def per_slot(counts, *shape):
        return [dma((c,) + shape) for c in counts]

    outs = (
        jax.ShapeDtypeStruct(g.shape, BF16),
        jax.ShapeDtypeStruct(share, F32),
        jax.ShapeDtypeStruct(share, F32),
    )
    gathered, first, second = pl.pallas_call(
        functools.partial(kernel, n, m),
        out_shape=outs,
        in_specs=[smem, hbm, hbm, hbm, hbm],
        out_specs=(anywhere, anywhere, anywhere),
        scratch_shapes=[
            pltpu.VMEM((mats, chips, piece, cols), BF16),
            pltpu.VMEM((mats, chips, piece, cols), BF16),
            pltpu.VMEM((mats, chips, piece, cols), BF16),
            pltpu.VMEM((mats, chips, piece, cols), BF16),
            pltpu.VMEM((chips, mats, piece, cols), BF16),
            pltpu.VMEM((chips - 1, mats, piece, cols), BF16),
            pltpu.VMEM((2, mats, piece, cols), BF16),
            pltpu.VMEM((mats, piece, cols), BF16),
            pltpu.VMEM((cap, m, piece, cols), BF16),
            pltpu.VMEM((cap, chips, piece, cols), BF16),
            pltpu.VMEM((cap, chips, piece, rank), BF16),
            pltpu.VMEM((2, cap, chips, rank_rows, cols), BF16),
            pltpu.VMEM((cap, chips, rank_rows, cols), BF16),
            pltpu.VMEM((cap, chips, rank_rows, cols), BF16),
            pltpu.VMEM((cap, chips - 1, rank_rows, cols), BF16),
            pltpu.VMEM((cap, n, 2, rank_rows, cols), BF16),
            pltpu.VMEM((cap, chips, piece, cols), BF16),
            pltpu.VMEM((cap, chips, piece, cols), BF16),
            [[pltpu.VMEM((m, piece // BACK_CHUNKS, cols), BF16)] * BACK_CHUNKS] * cap,
            pltpu.VMEM((mats, piece, cols), BF16),
            pltpu.VMEM((2, cap, rank_rows, cols), F32),
            pltpu.VMEM((2, cap, rank_rows, cols), F32),
            dma((5,)), dma((2, cap)), per_slot(bc),
            per_slot(oc), per_slot(oc),
            per_slot(oc, chips + 2), per_slot(oc, chips + 2),
            per_slot(oc, m), per_slot(oc, chips),
            dma((cap,)), dma((cap,)),
            dma((cap, chips)), dma((cap, chips)),
            dma((cap, chips)), dma((cap, chips)),
            dma((cap, chips)), dma((cap, chips)),
            per_slot(bc, chips), per_slot(bc, chips),
            per_slot(bc, m), per_slot(bc, m),
            per_slot(bc, chips), per_slot(bc, chips),
            per_slot(bc, chips), per_slot(bc, chips),
            per_slot(bc, chips), per_slot(bc, chips),
        ],
        compiler_params=pltpu.CompilerParams(
            collective_id=0, has_side_effects=True, vmem_limit_bytes=44 * 2**20
        ),
    )(*(pltpu.with_memory_space_constraint(x, pltpu.HBM) for x in (plan, g, w, moment1[0], moment2[0])))
    update, first, second = pl.pallas_call(
        settle,
        out_shape=outs,
        in_specs=[smem, anywhere, anywhere, anywhere],
        out_specs=(anywhere, anywhere, anywhere),
        scratch_shapes=[dma((mats + 2,))],
        compiler_params=pltpu.CompilerParams(vmem_limit_bytes=2**20),
    )(pltpu.with_memory_space_constraint(plan, pltpu.HBM), gathered, first, second)
    return (update.reshape(mats, own_rows, cols), first[None], second[None])


def solution(mesh):
    return jax.shard_map(
        local,
        mesh=mesh,
        in_specs=(
            P("dp", None, "own", None),
            P("own", None, "dp", None),
            P("own", None, "dp", None),
            P("own", None, "dp", None),
            P(),
        ),
        out_specs=(P(None, "own", None), P("own", None, "dp", None), P("own", None, "dp", None)),
        check_vma=False,
    )
```
